32 devices in a mesh: row: 4 (over z), col: 8 (over y, x, core).
Axes of the slice: x: 2, y: 2, z: 4, core: 2. Of those that a mesh axis runs over, the one named last changes fastest.
Arguments:
- species: float32 [53, 32, 64, 256], P(None, 'row', 'col'), may hold values from 0.05 to 2
- velocity: float32 [3, 32, 64, 256], P(None, 'row', 'col'), may hold values from -1 to 1
- diffusivity: float32 [53], replicated, may hold values from 0.02 to 0.1
- divergence: float32 [32, 64, 256], P('row', 'col'), may hold values from -6 to 6
- log_rates: float32 [325], replicated, may hold values from -3 to 1
- reactants: int32 [325, 53], replicated, may hold values from 0 to 3, as said below
- products: int32 [325, 53], replicated, may hold values from 0 to 3, as said below
- heat_weights: float32 [53], replicated, may hold values from -0.875 to 0.875
- substeps: int32 [32, 64, 2], P('row', 'col'), may hold values from 1 to 6
Outputs:
- reacted: float32 [53, 32, 64, 256], P(None, 'row', 'col')
- pressure: float32 [32, 64, 256], P('row', 'col')
The draws below stay inside these ranges and needn't reach their ends.
Inputs may be any that keep to these rules, and one draw needn't show every extreme that they name: `reactants`: each reaction has one or two reactant species. `products`: each reaction has one or two product species.
All inputs are finite; a program needn't handle non-finite values.
Results may differ from the reference program's by a relative error of at most 0.0003.
Values sent between devices are 32-bit elements; how exact they have to be, the bound alone decides.
No kernel may reach another device: no remote copies, remote signals or barrier semaphores. Data moves between devices by JAX's collectives and lax.ppermute only.
A program may use at most 128 MiB of HBM per device.

```python
import math
import jax
import jax.numpy as jnp
from jax import lax

NS = 53
NR = 325
NZ = 256
BLOCK = 128
MAXSUB = 6
NX = 32
NY = 64


def stoich_matrix(key):
    key_first, key_second, key_lead, key_extra = jax.random.split(key, 4)
    first = jax.random.randint(key_first, (NR,), 0, NS)
    second = jax.random.randint(key_second, (NR,), 0, NS)
    lead_coef = jax.random.randint(key_lead, (NR,), 1, 3)
    extra_coef = jax.random.randint(key_extra, (NR,), 0, 2)
    columns = jnp.arange(NS, dtype=jnp.int32)
    matrix = lead_coef[:, None] * (columns[None, :] == first[:, None]).astype(jnp.int32)
    matrix = matrix + extra_coef[:, None] * (columns[None, :] == second[:, None]).astype(jnp.int32)
    return matrix.astype(jnp.int32)


def draw_reactants(key, part):
    return stoich_matrix(jax.random.fold_in(key, 11))


def draw_products(key, part):
    return stoich_matrix(jax.random.fold_in(key, 23))


def draw_substeps(key, part):
    own_key = jax.random.fold_in(key, 37)
    key_front, key_heavy, key_light = jax.random.split(own_key, 3)
    front_start = jax.random.randint(key_front, (), 0, NX)
    position = jnp.arange(NX, dtype=jnp.int32)
    distance = jnp.mod(position - front_start, NX)
    inside = (distance < NX // 4)[:, None, None]
    heavy = jax.random.randint(key_heavy, (NX, NY, NZ // BLOCK), 4, 7)
    light = jax.random.randint(key_light, (NX, NY, NZ // BLOCK), 1, 3)
    return jnp.where(inside, heavy, light).astype(jnp.int32)


def block_scale(key, dims, cuts, least, high):
    def one(dim, shards_of):
        heights = jax.random.uniform(jax.random.fold_in(jax.random.fold_in(key, 6), dim), (shards_of,), jnp.float32, least / len(cuts), high / len(cuts))
        return jnp.repeat(jnp.exp(heights), dims[dim] // shards_of).reshape((-1,) + (1,) * (len(dims) - dim - 1))

    level = one(*cuts[0])
    for cut in cuts[1:]:
        level = level * one(*cut)
    return level


def scatter_about(stream_key, shape, width, reach, cuts=(), held_as=jnp.bfloat16):
    drawn = jax.random.normal(stream_key, shape, jnp.float32) * width
    if len(cuts) > 0:
        drawn = block_scale(stream_key, shape, cuts, -0.22, 0.18) * drawn
    return jnp.clip(drawn, min=-reach, max=reach).astype(held_as)


def setup_inputs(seed: int = 0) -> dict:
    key_of = jax.random.split(jax.random.key(seed), 10)
    return {
        "species": jnp.clip(jnp.exp(math.log(2.0) - 3.6888794 * jax.random.uniform(key_of[0], (NS, NX, NY, NZ), jnp.float32) ** block_scale(key_of[0], (NS, NX, NY, NZ), ((1, 4), (2, 8)), -0.2, 0.2)), 0.05, 2.0),
        "velocity": jnp.clip(jax.random.uniform(key_of[1], (3, NX, NY, NZ), jnp.float32, -1.0, 1.0) * block_scale(key_of[1], (3, NX, NY, NZ), ((1, 4), (2, 8)), -0.4, 0.0), -1.0, 1.0),
        "diffusivity": jnp.clip(jnp.exp(jax.random.uniform(key_of[2], (NS,), jnp.float32, math.log(0.02), math.log(0.1))), 0.02, 0.1),
        "divergence": scatter_about(key_of[3], (NX, NY, NZ), 1.0, 6.0, ((0, 4), (1, 8)), jnp.float32),
        "log_rates": jnp.clip(jax.random.uniform(key_of[4], (NR,), jnp.float32, -3.0, 1.0), -3.0, 1.0),
        "reactants": draw_reactants(jax.random.fold_in(key_of[9], 71), 0),
        "products": draw_products(jax.random.fold_in(key_of[9], 71), 0),
        "heat_weights": scatter_about(key_of[7], (NS,), NS ** -0.5, 0.875, (), jnp.float32),
        "substeps": draw_substeps(jax.random.fold_in(key_of[9], 71), 0),
    }


time_step = 0.2
screen = 0.004
highest = lax.Precision.HIGHEST

def cosine_table(length):
    wave = jnp.arange(length, dtype=jnp.float32)
    sample = jnp.arange(length, dtype=jnp.float32) + 0.5
    weight = jnp.where(wave == 0, jnp.sqrt(1.0 / length), jnp.sqrt(2.0 / length)).astype(jnp.float32)
    return weight[:, None] * jnp.cos(jnp.pi * wave[:, None] * sample[None, :] / length)

def mode_values(length):
    wave = jnp.arange(length, dtype=jnp.float32)
    return 2.0 - 2.0 * jnp.cos(jnp.pi * wave / length)

def transport(centre, padded, velocity, diffusivity):
    x_minus = padded[:, :-2, 1:-1, 1:-1]
    x_plus = padded[:, 2:, 1:-1, 1:-1]
    y_minus = padded[:, 1:-1, :-2, 1:-1]
    y_plus = padded[:, 1:-1, 2:, 1:-1]
    z_minus = padded[:, 1:-1, 1:-1, :-2]
    z_plus = padded[:, 1:-1, 1:-1, 2:]
    lateral = x_minus + x_plus + (y_minus + y_plus) + (z_minus + z_plus) - 6.0 * centre
    upwind = jnp.maximum(velocity, 0.0)[:, None]
    downwind = jnp.minimum(velocity, 0.0)[:, None]
    carried = upwind[0] * (centre - x_minus) + downwind[0] * (x_plus - centre)
    carried = carried + upwind[1] * (centre - y_minus) + downwind[1] * (y_plus - centre)
    carried = carried + upwind[2] * (centre - z_minus) + downwind[2] * (z_plus - centre)
    return centre + time_step * (diffusivity[:, None, None, None] * lateral - carried)

def react_step(conc, step_size, log_rates, react_float, prod_float):
    rates = jnp.exp(log_rates[:, None] + jnp.dot(react_float, jnp.log(conc), precision=highest, preferred_element_type=jnp.float32))
    gained = jnp.dot(prod_float.T, rates, precision=highest, preferred_element_type=jnp.float32)
    lost = jnp.dot(react_float.T, rates, precision=highest, preferred_element_type=jnp.float32)
    return conc * (conc + step_size * gained) / (conc + step_size * lost)

def reference(species, velocity, diffusivity, divergence, log_rates, reactants, products, heat_weights, substeps):
    padded = jnp.pad(species, ((0, 0), (1, 1), (1, 1), (1, 1)), mode='edge')
    moved = transport(species, padded, velocity, diffusivity)
    react_float = reactants.astype(jnp.float32)
    prod_float = products.astype(jnp.float32)
    per_cell = jnp.broadcast_to(substeps[:, :, :, None], (NX, NY, NZ // BLOCK, BLOCK)).reshape(NX, NY * NZ)
    step_cells = time_step / per_cell.astype(jnp.float32)
    stacked = jnp.transpose(moved.reshape(NS, NX, NY * NZ), (1, 0, 2))

    def one_slice(packed):
        conc, counts, sizes = packed
        for level in range(MAXSUB):
            fresh = react_step(conc, sizes[None, :], log_rates, react_float, prod_float)
            conc = jnp.where(counts[None, :] > level, fresh, conc)
        return conc
    result = lax.map(one_slice, (stacked, per_cell, step_cells))
    reacted = jnp.transpose(result, (1, 0, 2)).reshape(NS, NX, NY, NZ)
    heat = jnp.einsum('s,sxyz->xyz', heat_weights, reacted - moved, precision=highest) / time_step
    source = divergence - heat
    table_x = cosine_table(NX)
    table_y = cosine_table(NY)
    table_z = cosine_table(NZ)
    spectrum = jnp.einsum('cz,xyz->xyc', table_z, source, precision=highest)
    spectrum = jnp.einsum('ax,xyc->ayc', table_x, spectrum, precision=highest)
    spectrum = jnp.einsum('by,ayc->abc', table_y, spectrum, precision=highest)
    denominator = screen + mode_values(NX)[:, None, None] + mode_values(NY)[None, :, None] + mode_values(NZ)[None, None, :]
    spectrum = spectrum / denominator
    spectrum = jnp.einsum('by,abc->ayc', table_y, spectrum, precision=highest)
    spectrum = jnp.einsum('ax,ayc->xyc', table_x, spectrum, precision=highest)
    pressure = jnp.einsum('cz,xyc->xyz', table_z, spectrum, precision=highest)
    return (reacted, pressure)
```

```python
import functools
import math

import jax
import jax.numpy as jnp
import numpy as np
from jax import lax
from jax.experimental import pallas as pl
from jax.experimental.pallas import tpu as pltpu
from jax.sharding import PartitionSpec as P

BLOCK = 128
MAXSUB = 6
LANES = 128
TILE = 8

time_step = 0.2
screen = 0.004
log2e = 1.4426950408889634
f32 = jnp.float32
bf16 = jnp.bfloat16


def round_up(value, multiple):
    return -(-value // multiple) * multiple


def cosine_table(length):
    wave = np.arange(length, dtype=np.float64)
    weight = np.where(wave == 0, math.sqrt(1.0 / length), math.sqrt(2.0 / length))
    table = weight[:, None] * np.cos(math.pi * wave[:, None] * (wave[None, :] + 0.5) / length)
    return table.astype(np.float32)


def mode_values(length):
    wave = np.arange(length, dtype=np.float64)
    return 2.0 - 2.0 * np.cos(math.pi * wave / length)


def halves(value):
    high = value.astype(bf16)
    return high, (value - high.astype(f32)).astype(bf16)


def dot3(left, right, dims=((1,), (0,))):
    left_high, left_low = halves(left)
    right_high, right_low = halves(right)

    def product(a, b):
        return lax.dot_general(a, b, (dims, ((), ())), preferred_element_type=f32)

    small = product(left_low, right_high) + product(left_high, right_low)
    return product(left_high, right_high) + small


def transport_weights(velocity):
    ups = [time_step * jnp.maximum(v, 0.0) for v in velocity]
    downs = [-time_step * jnp.minimum(v, 0.0) for v in velocity]
    own = 1.0
    for weight in ups + downs:
        own = own - weight
    return ups, downs, own


def z_neighbours(tiles):
    lane = lax.broadcasted_iota(jnp.int32, (TILE, LANES), 1)
    up = [pltpu.roll(t, 1, 1) for t in tiles]
    down = [pltpu.roll(t, LANES - 1, 1) for t in tiles]
    minus, plus = [], []
    last = len(tiles) - 1
    for i, tile in enumerate(tiles):
        minus.append(jnp.where(lane == 0, tile if i == 0 else up[i - 1], up[i]))
        plus.append(jnp.where(lane == LANES - 1, tile if i == last else down[i + 1], down[i]))
    return minus, plus


def sort_start(hist):
    for n in range(MAXSUB + 2):
        hist[n] = 0


def sort_count(i, total, table, substeps, hist):
    j = jnp.minimum(i, total - 1)
    n = substeps[table[j] >> 8]
    hist[n] = hist[n] + jnp.where(i < total, 1, 0)


def sort_offsets(hist):
    start = 0
    for n in range(MAXSUB, 0, -1):
        count = hist[n]
        hist[n] = start
        start = start + count


def sort_place(i, total, table, substeps, hist, order, sorted_counts):
    j = jnp.minimum(i, total - 1)
    code = table[j]
    n = substeps[code >> 8]
    place = jnp.where(i < total, hist[n], total)
    order[place] = code
    sorted_counts[place] = n
    hist[n] = hist[n] + jnp.where(i < total, 1, 0)


def react_blocks(total, group, refs):
    order, counts, steps, mv, conc, rp_ref, st_ref, heat, weight_ref = refs
    ns8 = conc.shape[0]
    pieces = st_ref.shape[1] // 2
    rows = rp_ref.shape[0]
    width = group * LANES

    def place_of(code):
        row = (code >> 1) & 7
        return (code >> 4) & 15, code & 1, pl.ds(row, ns8, stride=TILE)

    def one_group(g, carry):
        base = g * group
        codes = [order[base + i] for i in range(group)]
        ns = [counts[base + i] for i in range(group)]
        hs = [steps[n] for n in ns]
        most = ns[0]
        for i, code in enumerate(codes):
            plane, half, row = place_of(code)
            conc[:, i * LANES : (i + 1) * LANES] = mv[plane, half, row, :]

        def one_level(level, inner):
            held = conc[...]
            logs = jnp.log(held) * log2e
            high = logs.astype(bf16).astype(f32)
            low = logs - high
            fill = jnp.zeros((rp_ref.shape[1] - 2 * ns8, width), f32)
            stacked = jnp.concatenate([high, low, fill], axis=0).astype(bf16)
            rates = jnp.exp2(jnp.dot(rp_ref[...], stacked, preferred_element_type=f32))
            first, second = halves(rates)
            gap = jnp.zeros((pieces - rows, width), bf16)
            both = jnp.concatenate([first, gap, second, gap], axis=0)
            sums = jnp.dot(st_ref[...], both, preferred_element_type=f32)
            for i in range(group):
                part = slice(i * LANES, (i + 1) * LANES)
                old = held[:, part]
                fresh = old * (old + hs[i] * sums[:ns8, part]) / (old + hs[i] * sums[ns8:, part])
                conc[:, part] = jnp.where(ns[i] > level, fresh, old)
            return inner

        lax.fori_loop(0, most, one_level, 0)
        for i, code in enumerate(codes):
            plane, half, row = place_of(code)
            new = conc[:, i * LANES : (i + 1) * LANES]
            change = (new - mv[plane, half, row, :]) * weight_ref[...]
            heat[half, pl.ds(code >> 9, 1), :] = jnp.sum(change, axis=0, keepdims=True)
            mv[plane, half, row, :] = new
        return carry

    lax.fori_loop(0, total // group, one_group, 0)


def inner_kernel(
    dims,
    group,
    table,
    substeps,
    steps,
    diffusivity,
    species_hbm,
    velocity,
    log_rates,
    reactants,
    products,
    heat_weights,
    mv_hbm,
    heat,
    rp_ref,
    st_ref,
    weight_ref,
    sp,
    mv,
    conc,
    build,
    hist,
    order,
    counts,
    in_sem,
    out_sem,
):
    ns, cx, cy, halves_z = dims
    nr = log_rates.shape[1]
    ns8 = conc.shape[0]
    total = 2 * (cx - 2) * (cy - 2)
    flat = sp.reshape(halves_z, ns * cx * cy, LANES)

    def load(x, z):
        return pltpu.make_async_copy(
            species_hbm.at[:, x, :, pl.ds(z * LANES, LANES)], sp.at[z, :, x], in_sem.at[x, z]
        )

    for x in range(cx):
        for z in range(halves_z):
            load(x, z).start()

    react = reactants[...].astype(f32)
    build[...] = jnp.zeros_like(build)
    build[0:ns, 0:nr] = react
    build[ns8 : ns8 + ns, 0:nr] = react
    rest = log_rates[...] * log2e
    for i in range(3):
        piece = rest.astype(bf16).astype(f32)
        build[ns + i : ns + i + 1, 0:nr] = piece
        rest = rest - piece
    rp_ref[...] = build[...].T[: rp_ref.shape[0]].astype(bf16)
    build[...] = jnp.zeros_like(build)
    build[0:ns, 0:nr] = products[...].astype(f32)
    build[ns8 : ns8 + ns, 0:nr] = react
    half = build[0 : 2 * ns8, :].astype(bf16)
    st_ref[...] = jnp.concatenate([half, half], axis=1)
    build[...] = jnp.zeros_like(build)
    build[:, 0:ns] = jnp.broadcast_to(heat_weights[...], (build.shape[0], ns))
    weight_ref[...] = build[:, 0:LANES].T[:ns8]
    mv[:, :, ns * TILE :, :] = jnp.full(
        (mv.shape[0], halves_z, (ns8 - ns) * TILE, LANES), 2.0, f32
    )
    sort_start(hist)
    sublane = lax.broadcasted_iota(jnp.int32, (TILE, LANES), 0)

    def run_plane(slot, weights, tile_of, side):
        unroll = 4

        def step(i, carry):
            for j in range(unroll):
                s = jnp.minimum(i * unroll + j, ns - 1)
                d = time_step * diffusivity[s]
                got = [tile_of(s, z) for z in range(halves_z)]
                zm, zp = z_neighbours([g[0] for g in got])
                for z in range(halves_z):
                    c = got[z][0]
                    ups, downs, own = weights[z]
                    sides = [*got[z][1:], zm[z], zp[z]]
                    wanted = [ups[0], downs[0], ups[1], downs[1], ups[2], downs[2]]
                    value = own * c
                    near = -6.0 * c
                    for w, t in zip(wanted, sides):
                        if t is None:
                            continue
                        value = value + w * t
                        near = near + t
                    mv[slot, z, pl.ds(s * TILE, TILE), :] = value + d * near
                side(i * unroll + j)
            return carry

        lax.fori_loop(0, -(-ns // unroll), step, 0)

    def nothing(i):
        pass

    span = 4 * (-(-ns // 4))

    def wait(x):
        for z in range(halves_z):
            load(x, z).wait()

    wait(0)
    wait(1)
    for x in range(1, cx - 1):
        wait(x + 1)
        lanes = [pl.ds(z * LANES, LANES) for z in range(halves_z)]
        weights = [transport_weights([velocity[d, x, :, q] for d in range(3)]) for q in lanes]

        def tile_of(s, z, x=x):
            c = sp[z, s, x]
            return (c, sp[z, s, x - 1], sp[z, s, x + 1], pltpu.roll(c, 1, 0), pltpu.roll(c, TILE - 1, 0))

        slot = x - 1
        if slot * span < total:
            side = lambda i, o=slot * span: sort_count(i + o, total, table, substeps, hist)
        elif (slot - 3) * span < total and slot >= 3:
            if slot == 3:
                sort_offsets(hist)
            side = lambda i, o=(slot - 3) * span: sort_place(
                i + o, total, table, substeps, hist, order, counts
            )
        else:
            side = nothing
        run_plane(slot, weights, tile_of, side)
    for slot, x, inward in ((cx - 2, 0, 1), (cx - 1, cx - 1, -1)):
        weights = []
        for z in range(halves_z):
            weights.append(
                transport_weights([velocity[d, x, :, pl.ds(z * LANES, LANES)] for d in range(3)])
            )

        def tile_of(s, z, x=x, inward=inward):
            c = sp[z, s, x]
            inner = sp[z, s, x + inward]
            ym = jnp.where(sublane == 0, 0.0, pltpu.roll(c, 1, 0))
            yp = jnp.where(sublane == TILE - 1, 0.0, pltpu.roll(c, TILE - 1, 0))
            if inward > 0:
                return c, None, inner, ym, yp
            return c, inner, None, ym, yp

        run_plane(slot, weights, tile_of, nothing)
    for slot, y, inward in ((cx, 0, 1), (cx + 1, cy - 1, -1)):
        weights = []
        for z in range(halves_z):
            q = pl.ds(z * LANES, LANES)
            weights.append(
                transport_weights(
                    [
                        jnp.concatenate([velocity[d, x, y : y + 1, q] for x in range(cx)], axis=0)
                        for d in range(3)
                    ]
                )
            )

        def tile_of(s, z, y=y, inward=inward):
            c = flat[z, pl.ds(s * cx * cy + y, cx, stride=cy), :]
            inner = flat[z, pl.ds(s * cx * cy + y + inward, cx, stride=cy), :]
            xm = pltpu.roll(c, 1, 0)
            xp = pltpu.roll(c, TILE - 1, 0)
            if inward > 0:
                return c, xm, xp, None, inner
            return c, xm, xp, inner, None

        run_plane(slot, weights, tile_of, nothing)

    def save(slot):
        return pltpu.make_async_copy(mv.at[slot], mv_hbm.at[slot], out_sem.at[slot])

    for slot in range(cx - 2, cx + 2):
        save(slot).start()
    react_blocks(
        total, group, (order, counts, steps, mv, conc, rp_ref, st_ref, heat, weight_ref)
    )
    for slot in range(cx - 2):
        save(slot).start()
    for slot in range(cx + 2):
        save(slot).wait()


def outer_kernel(
    dims,
    group,
    rows_count,
    cols_count,
    table,
    substeps,
    steps,
    diffusivity,
    velocity,
    divergence,
    mv_hbm,
    heat_inner,
    rp_ref,
    st_ref,
    weight_ref,
    table_z,
    own_x_low,
    own_x_high,
    own_y_low,
    own_y_high,
    got_x_low,
    got_x_high,
    got_y_low,
    got_y_high,
    reacted_hbm,
    forward,
    part,
    inner,
    mv,
    halo,
    stage,
    conc,
    heat,
    hist,
    order,
    counts,
    halo_sem,
    part_sem,
    inner_sem,
    out_sem,
):
    ns, cx, cy, halves_z = dims
    ns8 = conc.shape[0]
    total = 2 * (2 * cy + 2 * (cx - 2))
    row = lax.axis_index("row")
    col = lax.axis_index("col")
    walls = (row == 0, row == rows_count - 1, col == 0, col == cols_count - 1)
    own = (own_x_low, own_x_high, own_y_low, own_y_high)
    got = (got_x_low, got_x_high, got_y_low, got_y_high)
    for i in range(4):
        for z in range(halves_z):
            q = pl.ds(z * LANES, LANES)

            @pl.when(walls[i])
            def _(i=i, z=z, q=q):
                pltpu.make_async_copy(own[i].at[:, :, q], halo.at[i, z], halo_sem.at[i, z]).start()

            @pl.when(jnp.logical_not(walls[i]))
            def _(i=i, z=z, q=q):
                pltpu.make_async_copy(got[i].at[:, :, q], halo.at[i, z], halo_sem.at[i, z]).start()

    def load_part(slot):
        return pltpu.make_async_copy(mv_hbm.at[cx - 2 + slot], mv.at[slot], part_sem.at[slot])

    def load_inner(slot):
        return pltpu.make_async_copy(mv_hbm.at[slot], inner.at[slot], inner_sem.at[slot])

    for slot in range(4):
        load_part(slot).start()
    for slot in range(cx - 2):
        load_inner(slot).start()
    sort_start(hist)
    sublane = lax.broadcasted_iota(jnp.int32, (TILE, LANES), 0)
    heat[...] = heat_inner[...]
    for i in range(4):
        for z in range(halves_z):
            pltpu.make_async_copy(got[i].at[:, :, pl.ds(z * LANES, LANES)], halo.at[i, z], halo_sem.at[i, z]).wait()
    for slot in range(4):
        load_part(slot).wait()
    unroll = 4
    steps_s = -(-ns // unroll)
    span = unroll * steps_s
    for slot, x, y in ((0, 0, None), (1, cx - 1, None), (2, None, 0), (3, None, cy - 1)):
        weights = []
        for z in range(halves_z):
            q = pl.ds(z * LANES, LANES)
            if y is None:
                ups, downs, _ = transport_weights([velocity[d, x, :, q] for d in range(3)])
                low = jnp.where(sublane == 0, ups[1], 0.0)
                high = jnp.where(sublane == TILE - 1, downs[1], 0.0)
                weights.append((ups[0] if slot == 0 else downs[0], low, high))
            else:
                across = jnp.concatenate([velocity[1, i, y : y + 1, q] for i in range(cx)], axis=0)
                ups, downs, _ = transport_weights([across])
                weights.append((ups[0] if slot == 2 else downs[0],))
        at_low = jnp.where(sublane == 0, 1.0, 0.0)
        at_high = jnp.where(sublane == TILE - 1, 1.0, 0.0)
        if slot == 2:
            sort_offsets(hist)

        def step(i, carry, slot=slot, x=x, y=y, weights=weights):
            for j in range(unroll):
                s = jnp.minimum(i * unroll + j, ns - 1)
                valid = i * unroll + j < ns
                d = time_step * diffusivity[s]
                for z in range(halves_z):
                    rows = pl.ds(s * TILE, TILE)
                    value = mv[slot, z, rows, :] + (weights[z][0] + d) * halo[slot, z, s]
                    if y is None:
                        below = jnp.broadcast_to(halo[2, z, s, x : x + 1, :], (TILE, LANES))
                        above = jnp.broadcast_to(halo[3, z, s, x : x + 1, :], (TILE, LANES))
                        value = value + (weights[z][1] + d * at_low) * below
                        value = value + (weights[z][2] + d * at_high) * above
                    target = jnp.minimum(i * unroll + j, ns)
                    part[slot, z, pl.ds(target * TILE, TILE), :] = value
                at = i * unroll + j + (slot % 2) * span
                if slot < 2:
                    sort_count(at, total, table, substeps, hist)
                else:
                    sort_place(at, total, table, substeps, hist, order, counts)
            return carry

        lax.fori_loop(0, steps_s, step, 0)
    part[:, :, ns * TILE :, :] = jnp.full((4, halves_z, (ns8 - ns) * TILE, LANES), 2.0, f32)
    react_blocks(
        total, group, (order, counts, steps, part, conc, rp_ref, st_ref, heat, weight_ref)
    )
    for slot in range(cx - 2):
        load_inner(slot).wait()

    def save(x):
        return pltpu.make_async_copy(stage.at[x], reacted_hbm.at[:, x], out_sem.at[x])

    for x in range(cx):

        def fill(s, carry, x=x):
            for z in range(halves_z):
                q = pl.ds(z * LANES, LANES)
                rows = pl.ds(s * TILE, TILE)
                if x in (0, cx - 1):
                    tile = part[0 if x == 0 else 1, z, rows, :]
                else:
                    low = jnp.broadcast_to(part[2, z, pl.ds(s * TILE + x, 1), :], (TILE, LANES))
                    high = jnp.broadcast_to(part[3, z, pl.ds(s * TILE + x, 1), :], (TILE, LANES))
                    tile = jnp.where(sublane == 0, low, inner[x - 1, z, rows, :])
                    tile = jnp.where(sublane == TILE - 1, high, tile)
                stage[x, s, :, q] = tile
            return carry

        lax.fori_loop(0, ns, fill, 0)
        save(x).start()
    heat_all = jnp.concatenate([heat[z] for z in range(halves_z)], axis=1)
    source = divergence[...] - heat_all / time_step
    result = dot3(table_z[...], source, ((1,), (1,)))
    forward[...] = jnp.zeros_like(forward)
    forward[:, 0 : cx * cy] = result
    for x in range(cx):
        save(x).wait()


def solve_kernel(dims, lam_z, planes, table_y, mix_x, base, out, wide, tall):
    rows_count, cols_count, depth, cx, cy = dims
    cells = cx * cy
    nb = base.shape[1]
    na = rows_count * cx
    device = lax.axis_index("row") * cols_count + lax.axis_index("col")
    group = rows_count * depth
    total = jnp.zeros((group, cx * nb), f32)
    for c in range(cols_count):
        wide[c] = jnp.zeros((cells, cx * nb), f32)
        for x in range(cx):
            wide[c, x * cy : (x + 1) * cy, x * nb : (x + 1) * nb] = table_y[c * cy : (c + 1) * cy, :]
        if planes.ndim == 2:
            block = jnp.concatenate(
                [
                    planes[(r * cols_count + c) * depth : (r * cols_count + c + 1) * depth, 0:cells]
                    for r in range(rows_count)
                ],
                axis=0,
            )
        else:
            block = planes[c, :, 0:cells]
        total = total + dot3(block, wide[c])
    for x in range(cx):
        tall[x * group : (x + 1) * group, :] = total[:, x * nb : (x + 1) * nb]
    spectrum = dot3(mix_x[...], tall[...])
    solved = []
    for k in range(depth):
        rows = slice(k * na, (k + 1) * na)
        solved.append(spectrum[rows] / (base[...] + lam_z[device * depth + k]))
    spectrum = jnp.concatenate(solved, axis=0)
    back = dot3(mix_x[...], spectrum, ((0,), (0,)))
    row = jnp.concatenate([back[x * group : (x + 1) * group] for x in range(cx)], axis=1)
    out[...] = jnp.zeros_like(out)
    for c in range(cols_count):
        block = dot3(row, wide[c], ((1,), (1,)))
        if planes.ndim == 2:
            for r in range(rows_count):
                at = (r * cols_count + c) * depth
                out[at : at + depth, 0:cells] = block[r * depth : (r + 1) * depth]
        else:
            out[c, :, 0:cells] = block


def inverse_kernel(columns, table_z, out):
    cells = out.shape[0]
    out[...] = dot3(columns[...].T[:cells], table_z[...])


smem = pl.BlockSpec(memory_space=pltpu.SMEM)
vmem = pl.BlockSpec(memory_space=pltpu.VMEM)
anywhere = pl.BlockSpec(memory_space=pl.ANY)


def pick_group(total, most):
    best = 2
    for group in range(2, most + 1, 2):
        if total % group == 0:
            best = group
    return best


def local(
    species,
    velocity,
    diffusivity,
    divergence,
    log_rates,
    reactants,
    products,
    heat_weights,
    substeps,
):
    ns, cx, cy, nz = species.shape
    nr = log_rates.shape[0]
    rows_count = lax.axis_size("row")
    cols_count = lax.axis_size("col")
    device_count = rows_count * cols_count
    halves_z = nz // LANES
    ns8 = round_up(ns + 3, TILE)
    nr_rows = round_up(nr, 16)
    nr_lanes = round_up(nr, LANES)
    depth = nz // device_count
    cells = cx * cy
    dims = (ns, cx, cy, halves_z)

    own = (species[:, 0], species[:, cx - 1], species[:, :, 0], species[:, :, cy - 1])

    def shift(value, axis, step):
        count = lax.axis_size(axis)
        pairs = [(i, i + step) for i in range(count) if 0 <= i + step < count]
        return lax.ppermute(value, axis, pairs)

    got = (
        shift(own[1], "row", 1),
        shift(own[0], "row", -1),
        shift(own[3], "col", 1),
        shift(own[2], "col", -1),
    )

    def code(slot, row, x, y, half):
        flat = x * cy + y
        return (flat * 2 + half) << 8 | slot << 4 | row << 1 | half

    inner_codes = [
        code(x - 1, y, x, y, z) for x in range(1, cx - 1) for y in range(1, cy - 1) for z in range(halves_z)
    ]
    outer_columns = [(0, y, 0, y) for y in range(cy)] + [(1, y, cx - 1, y) for y in range(cy)]
    outer_columns += [(2, x, x, 0) for x in range(1, cx - 1)]
    outer_columns += [(3, x, x, cy - 1) for x in range(1, cx - 1)]
    outer_codes = [code(*column, z) for column in outer_columns for z in range(halves_z)]
    inner_table = jnp.asarray(np.array(inner_codes, np.int32))
    outer_table = jnp.asarray(np.array(outer_codes, np.int32))
    steps = jnp.asarray(
        np.array([0.0] + [np.float32(time_step) / np.float32(n) for n in range(1, 8)], np.float32)
    )
    flat_substeps = substeps.reshape(cells * halves_z)
    inner_total = len(inner_codes)
    outer_total = len(outer_codes)
    inner_group = pick_group(inner_total, 12)
    outer_group = pick_group(outer_total, 8)
    limit = pltpu.CompilerParams(vmem_limit_bytes=48 << 20)

    mv_shape = (cx + 2, halves_z, ns8 * TILE, LANES)
    mv_all, heat, rp, st, weight = pl.pallas_call(
        functools.partial(inner_kernel, dims, inner_group),
        out_shape=(
            jax.ShapeDtypeStruct(mv_shape, f32),
            jax.ShapeDtypeStruct((halves_z, cells, LANES), f32),
            jax.ShapeDtypeStruct((nr_rows, LANES), bf16),
            jax.ShapeDtypeStruct((2 * ns8, 2 * nr_lanes), bf16),
            jax.ShapeDtypeStruct((ns8, LANES), f32),
        ),
        in_specs=[smem, smem, smem, smem, anywhere, vmem, vmem, vmem, vmem, vmem],
        out_specs=(anywhere, vmem, vmem, vmem, vmem),
        scratch_shapes=[
            pltpu.VMEM((halves_z, ns, cx, cy, LANES), f32),
            pltpu.VMEM(mv_shape, f32),
            pltpu.VMEM((ns8, inner_group * LANES), f32),
            pltpu.VMEM((LANES, nr_lanes), f32),
            pltpu.SMEM((TILE,), jnp.int32),
            pltpu.SMEM((inner_total + 1,), jnp.int32),
            pltpu.SMEM((inner_total + 1,), jnp.int32),
            pltpu.SemaphoreType.DMA((cx, halves_z)),
            pltpu.SemaphoreType.DMA((cx + 2,)),
        ],
        compiler_params=limit,
        cost_estimate=pl.CostEstimate(
            flops=10**10, bytes_accessed=10**7, transcendentals=10**7
        ),
        name="inner",
    )(
        inner_table,
        flat_substeps,
        steps,
        diffusivity,
        species,
        velocity,
        log_rates[None, :],
        reactants.T,
        products.T,
        heat_weights[None, :],
    )
    table_z = jnp.asarray(cosine_table(nz))
    part_shape = (4, halves_z, ns8 * TILE, LANES)
    reacted, forward = pl.pallas_call(
        functools.partial(outer_kernel, dims, outer_group, rows_count, cols_count),
        out_shape=(
            jax.ShapeDtypeStruct(species.shape, f32),
            jax.ShapeDtypeStruct((nz, LANES), f32),
        ),
        in_specs=[smem] * 4 + [vmem, vmem, anywhere] + [vmem] * 5 + [anywhere] * 8,
        out_specs=(anywhere, vmem),
        scratch_shapes=[
            pltpu.VMEM(part_shape, f32),
            pltpu.VMEM((cx - 2, halves_z, ns8 * TILE, LANES), f32),
            pltpu.VMEM(part_shape, f32),
            pltpu.VMEM((4, halves_z, ns, TILE, LANES), f32),
            pltpu.VMEM((cx, ns, cy, nz), f32),
            pltpu.VMEM((ns8, outer_group * LANES), f32),
            pltpu.VMEM((halves_z, cells, LANES), f32),
            pltpu.SMEM((TILE,), jnp.int32),
            pltpu.SMEM((outer_total + 1,), jnp.int32),
            pltpu.SMEM((outer_total + 1,), jnp.int32),
            pltpu.SemaphoreType.DMA((4, halves_z)),
            pltpu.SemaphoreType.DMA((4,)),
            pltpu.SemaphoreType.DMA((cx - 2,)),
            pltpu.SemaphoreType.DMA((cx,)),
        ],
        compiler_params=limit,
        cost_estimate=pl.CostEstimate(
            flops=10**10, bytes_accessed=10**7, transcendentals=10**7
        ),
        name="outer",
    )(
        outer_table,
        flat_substeps,
        steps,
        diffusivity,
        velocity,
        divergence.reshape(cells, nz),
        mv_all,
        heat,
        rp,
        st,
        weight,
        table_z,
        *own,
        *got,
    )
    pressure = solve(forward, table_z, (rows_count, cols_count, depth, cx, cy))
    return reacted, pressure.reshape(cx, cy, nz)


def solve(forward, table_z, dims):
    rows_count, cols_count, depth, cx, cy = dims
    device_count = rows_count * cols_count
    nz = device_count * depth
    na, nb = rows_count * cx, cols_count * cy
    nb_pad = round_up(nb, LANES)
    aligned = depth % TILE == 0

    def exchange(value):
        value = value.reshape(device_count, depth, LANES)
        value = lax.all_to_all(value, ("row", "col"), split_axis=0, concat_axis=0, tiled=True)
        return value

    table_y = np.zeros((nb, nb_pad), np.float32)
    table_y[:, :nb] = cosine_table(nb).T
    table_x = cosine_table(na).reshape(na, rows_count, cx)
    mix_x = np.einsum("arx,kl->kaxrl", table_x, np.eye(depth, dtype=np.float32))
    mix_x = mix_x.reshape(depth * na, cx * rows_count * depth)
    base = np.full((na, nb_pad), 1.0, np.float64)
    base[:, :nb] = screen + mode_values(na)[:, None] + mode_values(nb)[None, :]
    planes = exchange(forward)
    group = rows_count * depth
    if aligned:
        planes = planes.reshape(nz, LANES)
        shape = (nz, LANES)
    else:
        planes = planes.reshape(rows_count, cols_count, depth, LANES).transpose(1, 0, 2, 3)
        shape = (cols_count, group, LANES)
        planes = planes.reshape(shape)
    outgoing = pl.pallas_call(
        functools.partial(solve_kernel, dims),
        out_shape=jax.ShapeDtypeStruct(shape, f32),
        in_specs=[smem, vmem, vmem, vmem, vmem],
        out_specs=vmem,
        scratch_shapes=[
            pltpu.VMEM((cols_count, cx * cy, cx * nb_pad), f32),
            pltpu.VMEM((cx * group, nb_pad), f32),
        ],
        compiler_params=pltpu.CompilerParams(vmem_limit_bytes=40 << 20),
        name="solve",
    )(
        jnp.asarray(mode_values(nz).astype(np.float32)),
        planes,
        jnp.asarray(table_y),
        jnp.asarray(mix_x),
        jnp.asarray(base.astype(np.float32)),
    )
    if not aligned:
        outgoing = outgoing.reshape(cols_count, rows_count, depth, LANES).transpose(1, 0, 2, 3)
    columns = exchange(outgoing).reshape(nz, LANES)
    return pl.pallas_call(
        inverse_kernel,
        out_shape=jax.ShapeDtypeStruct((cx * cy, nz), f32),
        in_specs=[vmem, vmem],
        out_specs=vmem,
        name="inverse",
    )(columns, table_z)


def solution(mesh):
    return jax.shard_map(
        local,
        mesh=mesh,
        in_specs=(
            P(None, "row", "col", None),
            P(None, "row", "col", None),
            P(),
            P("row", "col", None),
            P(),
            P(),
            P(),
            P(),
            P("row", "col", None),
        ),
        out_specs=(P(None, "row", "col", None), P("row", "col", None)),
        check_vma=False,
    )
```

```python
import functools
import math

import jax
import jax.numpy as jnp
import numpy as np
from jax import lax
from jax.experimental import pallas as pl
from jax.experimental.pallas import tpu as pltpu
from jax.sharding import PartitionSpec as P

BLOCK = 128
MAXSUB = 6
LANES = 128
TILE = 8

time_step = 0.2
screen = 0.004
log2e = 1.4426950408889634
f32 = jnp.float32
bf16 = jnp.bfloat16


def round_up(value, multiple):
    return -(-value // multiple) * multiple


def cosine_table(length):
    wave = np.arange(length, dtype=np.float64)
    weight = np.where(wave == 0, math.sqrt(1.0 / length), math.sqrt(2.0 / length))
    table = weight[:, None] * np.cos(math.pi * wave[:, None] * (wave[None, :] + 0.5) / length)
    return table.astype(np.float32)


def mode_values(length):
    wave = np.arange(length, dtype=np.float64)
    return 2.0 - 2.0 * np.cos(math.pi * wave / length)


def halves(value):
    high = value.astype(bf16)
    return high, (value - high.astype(f32)).astype(bf16)


def dot_halves(left, right, dims=((1,), (0,))):
    def product(a, b):
        return lax.dot_general(a, b, (dims, ((), ())), preferred_element_type=f32)

    small = product(left[1], right[0]) + product(left[0], right[1])
    return product(left[0], right[0]) + small


def dot3(left, right, dims=((1,), (0,))):
    return dot_halves(halves(left), halves(right), dims)


def transport_weights(velocity):
    ups = [time_step * jnp.maximum(v, 0.0) for v in velocity]
    downs = [-time_step * jnp.minimum(v, 0.0) for v in velocity]
    own = 1.0
    for weight in ups + downs:
        own = own - weight
    return ups, downs, own


def z_neighbours(tiles):
    lane = lax.broadcasted_iota(jnp.int32, (TILE, LANES), 1)
    up = [pltpu.roll(t, 1, 1) for t in tiles]
    down = [pltpu.roll(t, LANES - 1, 1) for t in tiles]
    minus, plus = [], []
    last = len(tiles) - 1
    for i, tile in enumerate(tiles):
        minus.append(jnp.where(lane == 0, tile if i == 0 else up[i - 1], up[i]))
        plus.append(jnp.where(lane == LANES - 1, tile if i == last else down[i + 1], down[i]))
    return minus, plus


def sort_blocks(substeps, codes, inner_first):
    blocks = substeps.shape[1]
    square = (blocks, blocks)
    key = jnp.broadcast_to(substeps + inner_first, square)
    key_down = key.T
    down = lax.broadcasted_iota(jnp.int32, square, 0)
    across = lax.broadcasted_iota(jnp.int32, square, 1)
    ahead = (key_down > key) | ((key_down == key) & (down < across))
    rank = jnp.sum(jnp.where(ahead, 1.0, 0.0), axis=0, keepdims=True)
    rank_down = jnp.broadcast_to(rank, square).T
    value_down = jnp.broadcast_to(codes * 8.0 + substeps, square).T
    chosen = jnp.where(rank_down == across.astype(f32), value_down, 0.0)
    return jnp.sum(chosen, axis=0, keepdims=True).astype(jnp.int32)


def react_blocks(first_block, total, group, refs, target_of):
    order, steps, mv, conc, rp_ref, st_ref, heat, weight_ref = refs
    ns8 = conc.shape[0]
    pieces = st_ref.shape[1] // 2
    rows = rp_ref.shape[0]
    width = group * LANES

    def spread(row):
        return pl.ds(row, ns8, stride=TILE)

    def one_group(g, carry):
        base = first_block + g * group
        values = [order[0, base + i] for i in range(group)]
        ns = [value & 7 for value in values]
        hs = [steps[n] for n in ns]
        places = []
        for value in values:
            code = value >> 3
            places.append(((code >> 4) & 15, code & 1, (code >> 1) & 7, code >> 9))
        for i, (plane, half, row, _) in enumerate(places):
            conc[:, i * LANES : (i + 1) * LANES] = mv[plane, half, spread(row), :]

        def one_level(level, inner):
            held = conc[...]
            logs = jnp.log(held) * log2e
            high = logs.astype(bf16).astype(f32)
            low = logs - high
            fill = jnp.zeros((rp_ref.shape[1] - 2 * ns8, width), f32)
            stacked = jnp.concatenate([high, low, fill], axis=0).astype(bf16)
            rates = jnp.exp2(jnp.dot(rp_ref[...], stacked, preferred_element_type=f32))
            first, second = halves(rates)
            gap = jnp.zeros((pieces - rows, width), bf16)
            both = jnp.concatenate([first, gap, second, gap], axis=0)
            sums = jnp.dot(st_ref[...], both, preferred_element_type=f32)
            for i in range(group):
                part = slice(i * LANES, (i + 1) * LANES)
                old = held[:, part]
                fresh = old * (old + hs[i] * sums[:ns8, part]) / (old + hs[i] * sums[ns8:, part])
                conc[:, part] = jnp.where(ns[i] > level, fresh, old)
            return inner

        lax.fori_loop(0, ns[0], one_level, 0)
        for i, (plane, half, row, column) in enumerate(places):
            new = conc[:, i * LANES : (i + 1) * LANES]
            change = (new - mv[plane, half, spread(row), :]) * weight_ref[...]
            heat[half, pl.ds(column, 1), :] = jnp.sum(change, axis=0, keepdims=True)
            to_plane, to_row = target_of(plane, row)
            mv[to_plane, half, spread(to_row), :] = new
        return carry

    lax.fori_loop(0, total // group, one_group, 0)


def over_species(ns, body, unroll=4):
    def step(i, carry):
        for j in range(unroll):
            body(i * unroll + j)
        return carry

    lax.fori_loop(0, ns // unroll, step, 0)
    for s in range(ns - ns % unroll, ns):
        body(s)


def prepare_kernel(
    dims,
    log_rates,
    substeps,
    species_hbm,
    velocity_hbm,
    diffusivity_hbm,
    reactants_hbm,
    products_hbm,
    weights_hbm,
    codes_hbm,
    sp,
    row_a,
    row_b,
    col_a,
    col_b,
    velocity,
    diffusivity,
    rp_ref,
    st_ref,
    weight_ref,
    order_row,
    build,
    reactants,
    products,
    heat_weights,
    codes,
    in_sem,
    small_sem,
):
    ns, cx, cy, halves_z = dims
    nr = log_rates.shape[1]
    ns8 = weight_ref.shape[0]

    def load(x, z):
        return pltpu.make_async_copy(
            species_hbm.at[:, x, :, pl.ds(z * LANES, LANES)], sp.at[z, :, x], in_sem.at[x, z]
        )

    small = [
        pltpu.make_async_copy(source, target, small_sem.at[i])
        for i, (source, target) in enumerate(
            (
                (reactants_hbm, reactants),
                (products_hbm, products),
                (weights_hbm, heat_weights),
                (codes_hbm, codes),
                (diffusivity_hbm, diffusivity),
                (velocity_hbm, velocity),
            )
        )
    ]
    for copy in small[:5]:
        copy.start()
    for x in range(cx):
        for z in range(halves_z):
            load(x, z).start()
    small[5].start()
    for copy in small[:5]:
        copy.wait()
    order_row[...] = sort_blocks(substeps[...].astype(f32), codes[0:1, :], codes[1:2, :])
    react = reactants[...].astype(f32)
    build[...] = jnp.zeros_like(build)
    build[0:ns, 0:nr] = react
    build[ns8 : ns8 + ns, 0:nr] = react
    rest = log_rates[...] * log2e
    for i in range(3):
        piece = rest.astype(bf16).astype(f32)
        build[ns + i : ns + i + 1, 0:nr] = piece
        rest = rest - piece
    rp_ref[...] = build[...].T[: rp_ref.shape[0]].astype(bf16)
    build[...] = jnp.zeros_like(build)
    build[0:ns, 0:nr] = products[...].astype(f32)
    build[ns8 : ns8 + ns, 0:nr] = react
    half = build[0 : 2 * ns8, :].astype(bf16)
    st_ref[...] = jnp.concatenate([half, half], axis=1)
    build[:, 0:LANES] = jnp.zeros((build.shape[0], LANES), f32)
    build[:, 0:ns] = jnp.broadcast_to(heat_weights[...], (build.shape[0], ns))
    weight_ref[...] = build[:, 0:LANES].T[:ns8]

    row_even = lax.rem(lax.axis_index("row"), 2) == 0
    col_even = lax.rem(lax.axis_index("col"), 2) == 0
    x_a = jnp.where(row_even, cx - 1, 0)
    y_a = jnp.where(col_even, cy - 1, 0)
    flat = sp.reshape(halves_z, ns * cx * cy, LANES)
    for x in range(cx):
        for z in range(halves_z):
            load(x, z).wait()

    def body(s):
        for z in range(halves_z):
            q = slice(z * LANES, (z + 1) * LANES)
            row_a[s, :, q] = sp[z, s, x_a]
            row_b[s, :, q] = sp[z, s, cx - 1 - x_a]
            col_a[s, :, q] = flat[z, pl.ds(s * cx * cy + y_a, cx, stride=cy), :]
            col_b[s, :, q] = flat[z, pl.ds(s * cx * cy + cy - 1 - y_a, cx, stride=cy), :]

    over_species(ns, body)
    small[5].wait()


def fill_steps(steps):
    steps[0] = 0.0
    for n in range(1, MAXSUB + 2):
        steps[n] = float(np.float32(time_step) / np.float32(n))


def inner_kernel(
    dims,
    total,
    group,
    order,
    diffusivity,
    sp,
    velocity,
    rp_ref,
    st_ref,
    weight_ref,
    mv,
    heat,
    conc,
    steps,
):
    ns, cx, cy, halves_z = dims
    ns8 = conc.shape[0]
    flat = sp.reshape(halves_z, ns * cx * cy, LANES)
    fill_steps(steps)
    mv[:, :, ns * TILE :, :] = jnp.full(
        (mv.shape[0], halves_z, (ns8 - ns) * TILE, LANES), 2.0, f32
    )
    heat[...] = jnp.zeros_like(heat)
    sublane = lax.broadcasted_iota(jnp.int32, (TILE, LANES), 0)

    def run_plane(slot, weights, tile_of):
        def body(s):
            d = time_step * diffusivity[0, s]
            got = [tile_of(s, z) for z in range(halves_z)]
            zm, zp = z_neighbours([g[0] for g in got])
            for z in range(halves_z):
                c = got[z][0]
                ups, downs, own = weights[z]
                sides = [*got[z][1:], zm[z], zp[z]]
                wanted = [ups[0], downs[0], ups[1], downs[1], ups[2], downs[2]]
                value = own * c
                near = -6.0 * c
                for w, t in zip(wanted, sides):
                    if t is None:
                        continue
                    value = value + w * t
                    near = near + t
                mv[slot, z, pl.ds(s * TILE, TILE), :] = value + d * near

        over_species(ns, body)

    lanes = [pl.ds(z * LANES, LANES) for z in range(halves_z)]
    for x in range(1, cx - 1):
        weights = [transport_weights([velocity[d, x, :, q] for d in range(3)]) for q in lanes]

        def tile_of(s, z, x=x):
            c = sp[z, s, x]
            return (
                c,
                sp[z, s, x - 1],
                sp[z, s, x + 1],
                pltpu.roll(c, 1, 0),
                pltpu.roll(c, TILE - 1, 0),
            )

        run_plane(x - 1, weights, tile_of)
    for slot, x, inward in ((cx - 2, 0, 1), (cx - 1, cx - 1, -1)):
        weights = []
        for q in lanes:
            ups, downs, own = transport_weights([velocity[d, x, :, q] for d in range(3)])
            weights.append((ups, downs, own))

        def tile_of(s, z, x=x, inward=inward):
            c = sp[z, s, x]
            inner = sp[z, s, x + inward]
            ym = jnp.where(sublane == 0, 0.0, pltpu.roll(c, 1, 0))
            yp = jnp.where(sublane == TILE - 1, 0.0, pltpu.roll(c, TILE - 1, 0))
            if inward > 0:
                return c, None, inner, ym, yp
            return c, inner, None, ym, yp

        run_plane(slot, weights, tile_of)
    for slot, y, inward in ((cx, 0, 1), (cx + 1, cy - 1, -1)):
        weights = []
        for q in lanes:
            rows = [
                jnp.concatenate([velocity[d, x, y : y + 1, q] for x in range(cx)], axis=0)
                for d in range(3)
            ]
            weights.append(transport_weights(rows))

        def tile_of(s, z, y=y, inward=inward):
            c = flat[z, pl.ds(s * cx * cy + y, cx, stride=cy), :]
            inner = flat[z, pl.ds(s * cx * cy + y + inward, cx, stride=cy), :]
            xm = pltpu.roll(c, 1, 0)
            xp = pltpu.roll(c, TILE - 1, 0)
            if inward > 0:
                return c, xm, xp, None, inner
            return c, xm, xp, inner, None

        run_plane(slot, weights, tile_of)
    refs = (order, steps, mv, conc, rp_ref, st_ref, heat, weight_ref)
    react_blocks(0, total, group, refs, lambda plane, row: (plane, row))


def outer_kernel(
    dims,
    first_block,
    total,
    group,
    rows_count,
    cols_count,
    order,
    diffusivity,
    velocity,
    divergence,
    mv_in,
    heat_inner,
    rp_ref,
    st_ref,
    weight_ref,
    table_z,
    row_sent_a,
    row_sent_b,
    col_sent_a,
    col_sent_b,
    row_got_a,
    row_got_b,
    col_got_a,
    col_got_b,
    reacted_hbm,
    forward,
    mv,
    table_high,
    table_low,
    halo,
    conc,
    heat,
    steps,
    halo_sem,
    out_sem,
):
    ns, cx, cy, halves_z = dims
    fill_steps(steps)
    row = lax.axis_index("row")
    col = lax.axis_index("col")
    lanes = [pl.ds(z * LANES, LANES) for z in range(halves_z)]

    def fetch(source, side):
        for z, q in enumerate(lanes):
            pltpu.make_async_copy(source.at[:, :, q], halo.at[side, z], halo_sem.at[side, z]).start()

    for axis, (at, count, sent, got) in enumerate(
        (
            (row, rows_count, (row_sent_a, row_sent_b), (row_got_a, row_got_b)),
            (col, cols_count, (col_sent_a, col_sent_b), (col_got_a, col_got_b)),
        )
    ):
        even = lax.rem(at, 2) == 0
        for side, wall, kinds in (
            (2 * axis, at == 0, (1, 0)),
            (2 * axis + 1, at == count - 1, (0, 1)),
        ):
            for parity, kind in zip((even, jnp.logical_not(even)), kinds):
                pl.when(parity & wall)(functools.partial(fetch, sent[kind], side))
                pl.when(parity & jnp.logical_not(wall))(
                    functools.partial(fetch, got[kind], side)
                )
    sublane = lax.broadcasted_iota(jnp.int32, (TILE, LANES), 0)
    at_low = jnp.where(sublane == 0, 1.0, 0.0)
    at_high = jnp.where(sublane == TILE - 1, 1.0, 0.0)
    heat[...] = heat_inner[...]

    def arrive(side):
        for z, q in enumerate(lanes):
            pltpu.make_async_copy(
                row_got_a.at[:, :, q], halo.at[side, z], halo_sem.at[side, z]
            ).wait()

    for side in range(4):
        arrive(side)
    base = cx - 2
    for slot, x, y in ((2, None, 0), (3, None, cy - 1), (0, 0, None), (1, cx - 1, None)):
        weights = []
        for q in lanes:
            if y is None:
                ups, downs, _ = transport_weights([velocity[d, x, :, q] for d in range(2)])
                low = jnp.where(sublane == 0, ups[1], 0.0)
                high = jnp.where(sublane == TILE - 1, downs[1], 0.0)
                weights.append((ups[0] if slot == 0 else downs[0], low, high))
            else:
                across = jnp.concatenate([velocity[1, i, y : y + 1, q] for i in range(cx)], axis=0)
                ups, downs, _ = transport_weights([across])
                weights.append((ups[0] if slot == 2 else downs[0],))

        def body(s, slot=slot, x=x, y=y, weights=weights):
            d = time_step * diffusivity[0, s]
            for z in range(halves_z):
                rows = pl.ds(s * TILE, TILE)
                value = mv[base + slot, z, rows, :] + (weights[z][0] + d) * halo[slot, z, s]
                if y is None:
                    below = jnp.broadcast_to(halo[2, z, s, x : x + 1, :], (TILE, LANES))
                    above = jnp.broadcast_to(halo[3, z, s, x : x + 1, :], (TILE, LANES))
                    value = value + (weights[z][1] + d * at_low) * below
                    value = value + (weights[z][2] + d * at_high) * above
                mv[base + slot, z, rows, :] = value

        over_species(ns, body)

    def target_of(plane, at_row):
        ours = plane < base + 2
        edge = jnp.where(plane == base + 2, 0, cy - 1)
        return jnp.where(ours, plane, at_row - 1), jnp.where(ours, at_row, edge)

    refs = (order, steps, mv, conc, rp_ref, st_ref, heat, weight_ref)
    react_blocks(first_block, total, group, refs, target_of)

    def save(x, z):
        plane = {0: base, cx - 1: base + 1}.get(x, x - 1)
        tiles = mv.reshape(cx + 2, halves_z, conc.shape[0], TILE, LANES)
        return pltpu.make_async_copy(
            tiles.at[plane, z, 0:ns], reacted_hbm.at[:, x, :, lanes[z]], out_sem.at[x, z]
        )

    for x in range(cx):
        for z in range(halves_z):
            save(x, z).start()
    heat_all = jnp.concatenate([heat[z] for z in range(halves_z)], axis=1)
    source = divergence[...] - heat_all / time_step
    table_high[...], table_low[...] = halves(table_z[...])
    result = dot_halves((table_high[...], table_low[...]), halves(source), ((1,), (1,)))
    forward[...] = jnp.zeros_like(forward)
    forward[:, 0 : cx * cy] = result
    for x in range(cx):
        for z in range(halves_z):
            save(x, z).wait()


def solve_kernel(dims, lam_z, planes, table_y, mix_x, base, out, wide, tall):
    rows_count, cols_count, depth, cx, cy = dims
    cells = cx * cy
    nb = base.shape[1]
    na = rows_count * cx
    device = lax.axis_index("row") * cols_count + lax.axis_index("col")
    group = rows_count * depth
    total = jnp.zeros((group, cx * nb), f32)
    for c in range(cols_count):
        wide[c] = jnp.zeros((cells, cx * nb), f32)
        for x in range(cx):
            wide[c, x * cy : (x + 1) * cy, x * nb : (x + 1) * nb] = table_y[c * cy : (c + 1) * cy, :]
        if planes.ndim == 2:
            block = jnp.concatenate(
                [
                    planes[(r * cols_count + c) * depth : (r * cols_count + c + 1) * depth, 0:cells]
                    for r in range(rows_count)
                ],
                axis=0,
            )
        else:
            block = planes[c, :, 0:cells]
        total = total + dot3(block, wide[c])
    for x in range(cx):
        tall[x * group : (x + 1) * group, :] = total[:, x * nb : (x + 1) * nb]
    spectrum = dot3(mix_x[...], tall[...])
    solved = []
    for k in range(depth):
        rows = slice(k * na, (k + 1) * na)
        solved.append(spectrum[rows] / (base[...] + lam_z[device * depth + k]))
    spectrum = jnp.concatenate(solved, axis=0)
    back = dot3(mix_x[...], spectrum, ((0,), (0,)))
    row = jnp.concatenate([back[x * group : (x + 1) * group] for x in range(cx)], axis=1)
    out[...] = jnp.zeros_like(out)
    for c in range(cols_count):
        block = dot3(row, wide[c], ((1,), (1,)))
        if planes.ndim == 2:
            for r in range(rows_count):
                at = (r * cols_count + c) * depth
                out[at : at + depth, 0:cells] = block[r * depth : (r + 1) * depth]
        else:
            out[c, :, 0:cells] = block


def inverse_kernel(columns, table_high, table_low, out):
    cells = out.shape[0]
    out[...] = dot_halves(halves(columns[...].T[:cells]), (table_high[...], table_low[...]))


smem = pl.BlockSpec(memory_space=pltpu.SMEM)
vmem = pl.BlockSpec(memory_space=pltpu.VMEM)
anywhere = pl.BlockSpec(memory_space=pl.ANY)
hbm = pl.BlockSpec(memory_space=pltpu.HBM)


def pick_group(total, most):
    best = 2
    for group in range(2, most + 1, 2):
        if total % group == 0:
            best = group
    return best


def local(
    species,
    velocity,
    diffusivity,
    divergence,
    log_rates,
    reactants,
    products,
    heat_weights,
    substeps,
):
    ns, cx, cy, nz = species.shape
    nr = log_rates.shape[0]
    rows_count = lax.axis_size("row")
    cols_count = lax.axis_size("col")
    device_count = rows_count * cols_count
    halves_z = nz // LANES
    ns8 = round_up(ns + 3, TILE)
    nr_rows = round_up(nr, 16)
    nr_lanes = round_up(nr, LANES)
    depth = nz // device_count
    cells = cx * cy
    dims = (ns, cx, cy, halves_z)

    codes = np.zeros((TILE, cells * halves_z), np.float32)
    inner_total = 0
    for x in range(cx):
        for y in range(cy):
            inside = 0 < x < cx - 1 and 0 < y < cy - 1
            if x in (0, cx - 1):
                slot, at = cx - 2 + (x > 0), y
            elif inside:
                slot, at = x - 1, y
            else:
                slot, at = cx + (y > 0), x
            for z in range(halves_z):
                flat = (x * cy + y) * halves_z + z
                codes[0, flat] = flat << 8 | slot << 4 | at << 1 | z
                codes[1, flat] = 8.0 * inside
                inner_total += inside
    outer_total = cells * halves_z - inner_total
    inner_group = pick_group(inner_total, 12)
    outer_group = pick_group(outer_total, 14)

    def array(*shape, dtype=f32):
        return jax.ShapeDtypeStruct(shape, dtype)

    mv_shape = (cx + 2, halves_z, ns8 * TILE, LANES)
    estimate = pl.CostEstimate(flops=10**10, bytes_accessed=10**7, transcendentals=10**7)
    sp, row_a, row_b, col_a, col_b, speed, spread, rp, st, weight, order = pl.pallas_call(
        functools.partial(prepare_kernel, dims),
        out_shape=(
            array(halves_z, ns, cx, cy, LANES),
            *(array(ns, TILE, nz),) * 4,
            array(*velocity.shape),
            array(1, ns),
            array(nr_rows, LANES, dtype=bf16),
            array(2 * ns8, 2 * nr_lanes, dtype=bf16),
            array(ns8, LANES),
            array(1, cells * halves_z, dtype=jnp.int32),
        ),
        in_specs=[vmem, vmem] + [hbm] * 7,
        out_specs=(vmem,) * 11,
        scratch_shapes=[
            pltpu.VMEM((LANES, nr_lanes), f32),
            pltpu.VMEM((ns, nr), jnp.int32),
            pltpu.VMEM((ns, nr), jnp.int32),
            pltpu.VMEM((1, ns), f32),
            pltpu.VMEM(codes.shape, f32),
            pltpu.SemaphoreType.DMA((cx, halves_z)),
            pltpu.SemaphoreType.DMA((6,)),
        ],
        compiler_params=pltpu.CompilerParams(vmem_limit_bytes=12 << 20),
        name="prepare",
    )(
        log_rates[None, :],
        substeps.reshape(1, cells * halves_z),
        *(
            pltpu.with_memory_space_constraint(value, pltpu.HBM)
            for value in (
                species,
                velocity,
                diffusivity[None, :],
                reactants.T,
                products.T,
                heat_weights[None, :],
                jnp.asarray(codes),
            )
        ),
    )
    sent = (row_a, row_b, col_a, col_b)

    def swap(value, axis, parity):
        pairs = []
        for low in range(parity, lax.axis_size(axis) - 1, 2):
            pairs += [(low, low + 1), (low + 1, low)]
        return lax.ppermute(value, axis, pairs)

    col_got = [swap(sent[2 + parity], "col", parity) for parity in range(2)]
    row_got = [swap(sent[parity], "row", parity) for parity in range(2)]
    got = (*row_got, *col_got)

    mv_all, heat = pl.pallas_call(
        functools.partial(inner_kernel, dims, inner_total, inner_group),
        out_shape=(array(*mv_shape), array(halves_z, cells, LANES)),
        in_specs=[smem, smem] + [vmem] * 5,
        out_specs=(vmem,) * 2,
        scratch_shapes=[
            pltpu.VMEM((ns8, inner_group * LANES), f32),
            pltpu.SMEM((MAXSUB + 2,), f32),
        ],
        compiler_params=pltpu.CompilerParams(vmem_limit_bytes=20 << 20),
        cost_estimate=estimate,
        name="inner",
    )(order, spread, sp, speed, rp, st, weight)
    table_z = jnp.asarray(cosine_table(nz))
    reacted, forward, _, *table_parts = pl.pallas_call(
        functools.partial(
            outer_kernel, dims, inner_total, outer_total, outer_group, rows_count, cols_count
        ),
        out_shape=(
            array(*species.shape),
            array(nz, LANES),
            array(*mv_shape),
            array(nz, nz, dtype=bf16),
            array(nz, nz, dtype=bf16),
        ),
        in_specs=[smem] * 2 + [vmem] * 8 + [anywhere] * 8,
        out_specs=(anywhere, vmem, vmem, vmem, vmem),
        scratch_shapes=[
            pltpu.VMEM((4, halves_z, ns, TILE, LANES), f32),
            pltpu.VMEM((ns8, outer_group * LANES), f32),
            pltpu.VMEM((halves_z, cells, LANES), f32),
            pltpu.SMEM((MAXSUB + 2,), f32),
            pltpu.SemaphoreType.DMA((4, halves_z)),
            pltpu.SemaphoreType.DMA((cx, halves_z)),
        ],
        input_output_aliases={4: 2},
        compiler_params=pltpu.CompilerParams(vmem_limit_bytes=20 << 20),
        cost_estimate=estimate,
        name="outer",
    )(
        order,
        spread,
        speed,
        divergence.reshape(cells, nz),
        mv_all,
        heat,
        rp,
        st,
        weight,
        table_z,
        *sent,
        *got,
    )
    pressure = solve(forward, table_parts, (rows_count, cols_count, depth, cx, cy))
    return reacted, pressure.reshape(cx, cy, nz)


def solve(forward, table_parts, dims):
    rows_count, cols_count, depth, cx, cy = dims
    device_count = rows_count * cols_count
    nz = device_count * depth
    na, nb = rows_count * cx, cols_count * cy
    nb_pad = round_up(nb, LANES)
    aligned = depth % TILE == 0

    def exchange(value):
        value = value.reshape(device_count, depth, LANES)
        value = lax.all_to_all(value, ("row", "col"), split_axis=0, concat_axis=0, tiled=True)
        return value

    table_y = np.zeros((nb, nb_pad), np.float32)
    table_y[:, :nb] = cosine_table(nb).T
    table_x = cosine_table(na).reshape(na, rows_count, cx)
    mix_x = np.einsum("arx,kl->kaxrl", table_x, np.eye(depth, dtype=np.float32))
    mix_x = mix_x.reshape(depth * na, cx * rows_count * depth)
    base = np.full((na, nb_pad), 1.0, np.float64)
    base[:, :nb] = screen + mode_values(na)[:, None] + mode_values(nb)[None, :]
    planes = exchange(forward)
    group = rows_count * depth
    if aligned:
        planes = planes.reshape(nz, LANES)
        shape = (nz, LANES)
    else:
        planes = planes.reshape(rows_count, cols_count, depth, LANES).transpose(1, 0, 2, 3)
        shape = (cols_count, group, LANES)
        planes = planes.reshape(shape)
    outgoing = pl.pallas_call(
        functools.partial(solve_kernel, dims),
        out_shape=jax.ShapeDtypeStruct(shape, f32),
        in_specs=[smem, vmem, vmem, vmem, vmem],
        out_specs=vmem,
        scratch_shapes=[
            pltpu.VMEM((cols_count, cx * cy, cx * nb_pad), f32),
            pltpu.VMEM((cx * group, nb_pad), f32),
        ],
        compiler_params=pltpu.CompilerParams(vmem_limit_bytes=40 << 20),
        name="solve",
    )(
        jnp.asarray(mode_values(nz).astype(np.float32)),
        planes,
        jnp.asarray(table_y),
        jnp.asarray(mix_x),
        jnp.asarray(base.astype(np.float32)),
    )
    if not aligned:
        outgoing = outgoing.reshape(cols_count, rows_count, depth, LANES).transpose(1, 0, 2, 3)
    columns = exchange(outgoing).reshape(nz, LANES)
    return pl.pallas_call(
        inverse_kernel,
        out_shape=jax.ShapeDtypeStruct((cx * cy, nz), f32),
        in_specs=[vmem] * 3,
        out_specs=vmem,
        name="inverse",
    )(columns, *table_parts)


def solution(mesh):
    return jax.shard_map(
        local,
        mesh=mesh,
        in_specs=(
            P(None, "row", "col", None),
            P(None, "row", "col", None),
            P(),
            P("row", "col", None),
            P(),
            P(),
            P(),
            P(),
            P("row", "col", None),
        ),
        out_specs=(P(None, "row", "col", None), P("row", "col", None)),
        check_vma=False,
    )
```

```python
import functools
import math

import jax
import jax.numpy as jnp
import numpy as np
from jax import lax
from jax.experimental import pallas as pl
from jax.experimental.pallas import tpu as pltpu
from jax.sharding import PartitionSpec as P

BLOCK = 128
MAXSUB = 6
LANES = 128
TILE = 8

time_step = 0.2
screen = 0.004
log2e = 1.4426950408889634
f32 = jnp.float32
bf16 = jnp.bfloat16


def round_up(value, multiple):
    return -(-value // multiple) * multiple


def cosine_table(length):
    wave = np.arange(length, dtype=np.float64)
    weight = np.where(wave == 0, math.sqrt(1.0 / length), math.sqrt(2.0 / length))
    table = weight[:, None] * np.cos(math.pi * wave[:, None] * (wave[None, :] + 0.5) / length)
    return table.astype(np.float32)


def mode_values(length):
    wave = np.arange(length, dtype=np.float64)
    return 2.0 - 2.0 * np.cos(math.pi * wave / length)


def halves(value):
    high = value.astype(bf16)
    return high, (value - high.astype(f32)).astype(bf16)


def dot_halves(left, right, dims=((1,), (0,))):
    def product(a, b):
        return lax.dot_general(a, b, (dims, ((), ())), preferred_element_type=f32)

    small = product(left[1], right[0]) + product(left[0], right[1])
    return product(left[0], right[0]) + small


def dot3(left, right, dims=((1,), (0,))):
    return dot_halves(halves(left), halves(right), dims)


def transport_weights(velocity):
    ups = [time_step * jnp.maximum(v, 0.0) for v in velocity]
    downs = [-time_step * jnp.minimum(v, 0.0) for v in velocity]
    own = 1.0
    for weight in ups + downs:
        own = own - weight
    return ups, downs, own


def z_neighbours(tiles):
    lane = lax.broadcasted_iota(jnp.int32, (TILE, LANES), 1)
    up = [pltpu.roll(t, 1, 1) for t in tiles]
    down = [pltpu.roll(t, LANES - 1, 1) for t in tiles]
    minus, plus = [], []
    last = len(tiles) - 1
    for i, tile in enumerate(tiles):
        minus.append(jnp.where(lane == 0, tile if i == 0 else up[i - 1], up[i]))
        plus.append(jnp.where(lane == LANES - 1, tile if i == last else down[i + 1], down[i]))
    return minus, plus


def sort_blocks(substeps, codes, inner_first):
    blocks = substeps.shape[1]
    square = (blocks, blocks)
    key = jnp.broadcast_to(substeps + inner_first, square)
    key_down = key.T
    down = lax.broadcasted_iota(jnp.int32, square, 0)
    across = lax.broadcasted_iota(jnp.int32, square, 1)
    ahead = (key_down > key) | ((key_down == key) & (down < across))
    rank = jnp.sum(jnp.where(ahead, 1.0, 0.0), axis=0, keepdims=True)
    rank_down = jnp.broadcast_to(rank, square).T
    value_down = jnp.broadcast_to(codes * 8.0 + substeps, square).T
    chosen = jnp.where(rank_down == across.astype(f32), value_down, 0.0)
    return jnp.sum(chosen, axis=0, keepdims=True).astype(jnp.int32)


def react_blocks(first_block, total, group, refs, target_of):
    order, steps, mv, conc, rp_ref, st_ref, heat, weight_ref = refs
    ns8 = conc.shape[0]
    pieces = st_ref.shape[1] // 2
    rows = rp_ref.shape[0]
    width = group * LANES

    def spread(row):
        return pl.ds(row, ns8, stride=TILE)

    def one_group(g, carry):
        base = first_block + g * group
        values = [order[0, base + i] for i in range(group)]
        ns = [value & 7 for value in values]
        hs = [steps[n] for n in ns]
        places = []
        for value in values:
            code = value >> 3
            places.append(((code >> 4) & 15, code & 1, (code >> 1) & 7, code >> 9))
        for i, (plane, half, row, _) in enumerate(places):
            conc[:, i * LANES : (i + 1) * LANES] = mv[plane, half, spread(row), :]

        def one_level(level, inner):
            held = conc[...]
            logs = jnp.log(held) * log2e
            high = logs.astype(bf16).astype(f32)
            low = logs - high
            fill = jnp.zeros((rp_ref.shape[1] - 2 * ns8, width), f32)
            stacked = jnp.concatenate([high, low, fill], axis=0).astype(bf16)
            rates = jnp.exp2(jnp.dot(rp_ref[...], stacked, preferred_element_type=f32))
            first, second = halves(rates)
            gap = jnp.zeros((pieces - rows, width), bf16)
            both = jnp.concatenate([first, gap, second, gap], axis=0)
            sums = jnp.dot(st_ref[...], both, preferred_element_type=f32)
            for i in range(group):
                part = slice(i * LANES, (i + 1) * LANES)
                old = held[:, part]
                fresh = old * (old + hs[i] * sums[:ns8, part]) / (old + hs[i] * sums[ns8:, part])
                conc[:, part] = jnp.where(ns[i] > level, fresh, old)
            return inner

        lax.fori_loop(0, ns[0], one_level, 0)
        for i, (plane, half, row, column) in enumerate(places):
            new = conc[:, i * LANES : (i + 1) * LANES]
            change = (new - mv[plane, half, spread(row), :]) * weight_ref[...]
            heat[half, pl.ds(column, 1), :] = jnp.sum(change, axis=0, keepdims=True)
            to_plane, to_row = target_of(plane, row)
            mv[to_plane, half, spread(to_row), :] = new
        return carry

    lax.fori_loop(0, total // group, one_group, 0)


def over_species(ns, body, unroll=18):
    def step(i, carry):
        for j in range(unroll):
            body(i * unroll + j)
        return carry

    lax.fori_loop(0, ns // unroll, step, 0)
    for s in range(ns - ns % unroll, ns):
        body(s)


def prepare_kernel(
    dims,
    species_hbm,
    velocity_hbm,
    diffusivity_hbm,
    reactants_hbm,
    products_hbm,
    weights_hbm,
    codes_hbm,
    rates_hbm,
    substeps_hbm,
    sp,
    row_a,
    row_b,
    col_a,
    col_b,
    velocity,
    diffusivity,
    rp_ref,
    st_ref,
    weight_ref,
    order_row,
    build,
    reactants,
    products,
    heat_weights,
    codes,
    log_rates,
    substeps,
    counts,
    in_sem,
    small_sem,
):
    ns, cx, cy, halves_z = dims
    nr = log_rates.shape[1]
    ns8 = weight_ref.shape[0]

    def load(x, z):
        return pltpu.make_async_copy(
            species_hbm.at[:, x, :, pl.ds(z * LANES, LANES)], sp.at[z, :, x], in_sem.at[x, z]
        )

    small = [
        pltpu.make_async_copy(source, target, small_sem.at[i])
        for i, (source, target) in enumerate(
            (
                (reactants_hbm, reactants),
                (products_hbm, products),
                (weights_hbm, heat_weights),
                (codes_hbm, codes),
                (diffusivity_hbm, diffusivity),
                (rates_hbm, log_rates),
                (substeps_hbm, substeps),
                (velocity_hbm, velocity),
            )
        )
    ]
    for copy in small[:-1]:
        copy.start()
    for x in range(cx):
        for z in range(halves_z):
            load(x, z).start()
    small[-1].start()
    for copy in small[:-1]:
        copy.wait()
    blocks = order_row.shape[1]
    counts[...] = jnp.zeros_like(counts)
    for x in range(cx):
        counts[x * halves_z : (x + 1) * halves_z, 0:cy] = substeps[x].astype(f32)
    down = lax.broadcasted_iota(jnp.int32, (LANES, blocks), 0)
    across = lax.broadcasted_iota(jnp.int32, (LANES, blocks), 1)
    repeat = jnp.where(lax.rem(across, cy) == down, 1.0, 0.0).astype(bf16)
    repeated = jnp.dot(counts[...].astype(bf16), repeat, preferred_element_type=f32)
    mine = lax.div(across, cy)[: counts.shape[0]] == down[: counts.shape[0]]
    flat_counts = jnp.sum(jnp.where(mine, repeated, 0.0), axis=0, keepdims=True)
    order_row[...] = sort_blocks(flat_counts, codes[0:1, :], codes[1:2, :])
    react = reactants[...].astype(f32)
    build[...] = jnp.zeros_like(build)
    build[0:ns, 0:nr] = react
    build[ns8 : ns8 + ns, 0:nr] = react
    rest = log_rates[...] * log2e
    for i in range(3):
        piece = rest.astype(bf16).astype(f32)
        build[ns + i : ns + i + 1, 0:nr] = piece
        rest = rest - piece
    rp_ref[...] = build[...].T[: rp_ref.shape[0]].astype(bf16)
    build[...] = jnp.zeros_like(build)
    build[0:ns, 0:nr] = products[...].astype(f32)
    build[ns8 : ns8 + ns, 0:nr] = react
    half = build[0 : 2 * ns8, :].astype(bf16)
    st_ref[...] = jnp.concatenate([half, half], axis=1)
    build[:, 0:LANES] = jnp.zeros((build.shape[0], LANES), f32)
    build[:, 0:ns] = jnp.broadcast_to(heat_weights[...], (build.shape[0], ns))
    weight_ref[...] = build[:, 0:LANES].T[:ns8]

    row_even = lax.rem(lax.axis_index("row"), 2) == 0
    col_even = lax.rem(lax.axis_index("col"), 2) == 0
    x_a = jnp.where(row_even, cx - 1, 0)
    y_a = jnp.where(col_even, cy - 1, 0)
    flat = sp.reshape(halves_z, ns * cx * cy, LANES)
    for x in range(cx):
        for z in range(halves_z):
            load(x, z).wait()

    def body(s):
        for z in range(halves_z):
            q = slice(z * LANES, (z + 1) * LANES)
            row_a[s, :, q] = sp[z, s, x_a]
            row_b[s, :, q] = sp[z, s, cx - 1 - x_a]
            col_a[s, :, q] = flat[z, pl.ds(s * cx * cy + y_a, cx, stride=cy), :]
            col_b[s, :, q] = flat[z, pl.ds(s * cx * cy + cy - 1 - y_a, cx, stride=cy), :]

    over_species(ns, body)
    small[-1].wait()


def fill_steps(steps):
    steps[0] = 0.0
    for n in range(1, MAXSUB + 2):
        steps[n] = float(np.float32(time_step) / np.float32(n))


def inner_kernel(
    dims,
    total,
    group,
    order,
    diffusivity,
    sp,
    velocity,
    rp_ref,
    st_ref,
    weight_ref,
    mv,
    heat,
    conc,
    steps,
):
    ns, cx, cy, halves_z = dims
    ns8 = conc.shape[0]
    flat = sp.reshape(halves_z, ns * cx * cy, LANES)
    fill_steps(steps)
    mv[:, :, ns * TILE :, :] = jnp.full(
        (mv.shape[0], halves_z, (ns8 - ns) * TILE, LANES), 2.0, f32
    )
    heat[...] = jnp.zeros_like(heat)
    sublane = lax.broadcasted_iota(jnp.int32, (TILE, LANES), 0)

    def run_plane(slot, weights, tile_of):
        def body(s):
            d = time_step * diffusivity[0, s]
            got = [tile_of(s, z) for z in range(halves_z)]
            zm, zp = z_neighbours([g[0] for g in got])
            for z in range(halves_z):
                c = got[z][0]
                ups, downs, own = weights[z]
                sides = [*got[z][1:], zm[z], zp[z]]
                wanted = [ups[0], downs[0], ups[1], downs[1], ups[2], downs[2]]
                value = own * c
                near = -6.0 * c
                for w, t in zip(wanted, sides):
                    if t is None:
                        continue
                    value = value + w * t
                    near = near + t
                mv[slot, z, pl.ds(s * TILE, TILE), :] = value + d * near

        over_species(ns, body)

    lanes = [pl.ds(z * LANES, LANES) for z in range(halves_z)]
    for x in range(1, cx - 1):
        weights = [transport_weights([velocity[d, x, :, q] for d in range(3)]) for q in lanes]

        def tile_of(s, z, x=x):
            c = sp[z, s, x]
            return (
                c,
                sp[z, s, x - 1],
                sp[z, s, x + 1],
                pltpu.roll(c, 1, 0),
                pltpu.roll(c, TILE - 1, 0),
            )

        run_plane(x - 1, weights, tile_of)
    for slot, x, inward in ((cx - 2, 0, 1), (cx - 1, cx - 1, -1)):
        weights = []
        for q in lanes:
            ups, downs, own = transport_weights([velocity[d, x, :, q] for d in range(3)])
            weights.append((ups, downs, own))

        def tile_of(s, z, x=x, inward=inward):
            c = sp[z, s, x]
            inner = sp[z, s, x + inward]
            ym = jnp.where(sublane == 0, 0.0, pltpu.roll(c, 1, 0))
            yp = jnp.where(sublane == TILE - 1, 0.0, pltpu.roll(c, TILE - 1, 0))
            if inward > 0:
                return c, None, inner, ym, yp
            return c, inner, None, ym, yp

        run_plane(slot, weights, tile_of)
    for slot, y, inward in ((cx, 0, 1), (cx + 1, cy - 1, -1)):
        weights = []
        for q in lanes:
            rows = [
                jnp.concatenate([velocity[d, x, y : y + 1, q] for x in range(cx)], axis=0)
                for d in range(3)
            ]
            weights.append(transport_weights(rows))

        def tile_of(s, z, y=y, inward=inward):
            c = flat[z, pl.ds(s * cx * cy + y, cx, stride=cy), :]
            inner = flat[z, pl.ds(s * cx * cy + y + inward, cx, stride=cy), :]
            xm = pltpu.roll(c, 1, 0)
            xp = pltpu.roll(c, TILE - 1, 0)
            if inward > 0:
                return c, xm, xp, None, inner
            return c, xm, xp, inner, None

        run_plane(slot, weights, tile_of)
    refs = (order, steps, mv, conc, rp_ref, st_ref, heat, weight_ref)
    react_blocks(0, total, group, refs, lambda plane, row: (plane, row))


def outer_kernel(
    dims,
    first_block,
    total,
    group,
    rows_count,
    cols_count,
    order,
    diffusivity,
    velocity,
    divergence,
    mv_in,
    heat_inner,
    rp_ref,
    st_ref,
    weight_ref,
    table_z,
    row_sent_a,
    row_sent_b,
    col_sent_a,
    col_sent_b,
    row_got_a,
    row_got_b,
    col_got_a,
    col_got_b,
    forward,
    mv,
    table_high,
    table_low,
    halo,
    conc,
    heat,
    steps,
    halo_sem,
):
    ns, cx, cy, halves_z = dims
    fill_steps(steps)
    row = lax.axis_index("row")
    col = lax.axis_index("col")
    lanes = [pl.ds(z * LANES, LANES) for z in range(halves_z)]

    def fetch(source, side):
        for z, q in enumerate(lanes):
            pltpu.make_async_copy(source.at[:, :, q], halo.at[side, z], halo_sem.at[side, z]).start()

    for axis, (at, count, sent, got) in enumerate(
        (
            (row, rows_count, (row_sent_a, row_sent_b), (row_got_a, row_got_b)),
            (col, cols_count, (col_sent_a, col_sent_b), (col_got_a, col_got_b)),
        )
    ):
        even = lax.rem(at, 2) == 0
        for side, wall, kinds in (
            (2 * axis, at == 0, (1, 0)),
            (2 * axis + 1, at == count - 1, (0, 1)),
        ):
            for parity, kind in zip((even, jnp.logical_not(even)), kinds):
                pl.when(parity & wall)(functools.partial(fetch, sent[kind], side))
                pl.when(parity & jnp.logical_not(wall))(
                    functools.partial(fetch, got[kind], side)
                )
    sublane = lax.broadcasted_iota(jnp.int32, (TILE, LANES), 0)
    at_low = jnp.where(sublane == 0, 1.0, 0.0)
    at_high = jnp.where(sublane == TILE - 1, 1.0, 0.0)
    heat[...] = heat_inner[...]

    def arrive(side):
        for z, q in enumerate(lanes):
            pltpu.make_async_copy(
                row_got_a.at[:, :, q], halo.at[side, z], halo_sem.at[side, z]
            ).wait()

    for side in range(4):
        arrive(side)
    base = cx - 2
    for slot, x, y in ((2, None, 0), (3, None, cy - 1), (0, 0, None), (1, cx - 1, None)):
        weights = []
        for q in lanes:
            if y is None:
                ups, downs, _ = transport_weights([velocity[d, x, :, q] for d in range(2)])
                low = jnp.where(sublane == 0, ups[1], 0.0)
                high = jnp.where(sublane == TILE - 1, downs[1], 0.0)
                weights.append((ups[0] if slot == 0 else downs[0], low, high))
            else:
                across = jnp.concatenate([velocity[1, i, y : y + 1, q] for i in range(cx)], axis=0)
                ups, downs, _ = transport_weights([across])
                weights.append((ups[0] if slot == 2 else downs[0],))

        def body(s, slot=slot, x=x, y=y, weights=weights):
            d = time_step * diffusivity[0, s]
            for z in range(halves_z):
                rows = pl.ds(s * TILE, TILE)
                value = mv[base + slot, z, rows, :] + (weights[z][0] + d) * halo[slot, z, s]
                if y is None:
                    below = jnp.broadcast_to(halo[2, z, s, x : x + 1, :], (TILE, LANES))
                    above = jnp.broadcast_to(halo[3, z, s, x : x + 1, :], (TILE, LANES))
                    value = value + (weights[z][1] + d * at_low) * below
                    value = value + (weights[z][2] + d * at_high) * above
                mv[base + slot, z, rows, :] = value

        over_species(ns, body)

    def target_of(plane, at_row):
        ours = plane < base + 2
        edge = jnp.where(plane == base + 2, 0, cy - 1)
        return jnp.where(ours, plane, at_row - 1), jnp.where(ours, at_row, edge)

    refs = (order, steps, mv, conc, rp_ref, st_ref, heat, weight_ref)
    react_blocks(first_block, total, group, refs, target_of)

    heat_all = jnp.concatenate([heat[z] for z in range(halves_z)], axis=1)
    source = divergence[...] - heat_all / time_step
    table_high[...], table_low[...] = halves(table_z[...])
    result = dot_halves((table_high[...], table_low[...]), halves(source), ((1,), (1,)))
    rows = forward.shape[0]
    sections = [result[i * rows : (i + 1) * rows] for i in range(LANES // (cx * cy))]
    forward[...] = jnp.concatenate(sections, axis=1)


def solve_kernel(
    dims, lam_z, planes, table_y, mix_x, base, mv, out, reacted_hbm, wide, tall, out_sem
):
    rows_count, cols_count, depth, cx, cy = dims
    ns, halves_z = reacted_hbm.shape[0], mv.shape[1]
    tiles = mv.reshape(*mv.shape[:2], mv.shape[2] // TILE, TILE, LANES)

    def save(x, z):
        plane = {0: cx - 2, cx - 1: cx - 1}.get(x, x - 1)
        return pltpu.make_async_copy(
            tiles.at[plane, z, 0:ns],
            reacted_hbm.at[:, x, :, pl.ds(z * LANES, LANES)],
            out_sem.at[x, z],
        )

    for x in range(cx):
        for z in range(halves_z):
            save(x, z).start()
    cells = cx * cy
    nb = base.shape[1]
    na = rows_count * cx
    sections = LANES // cells
    run = depth // sections
    device = lax.axis_index("row") * cols_count + lax.axis_index("col")
    group = rows_count * depth
    total = jnp.zeros((group, cx * nb), f32)
    for c in range(cols_count):
        wide[c] = jnp.zeros((cells, cx * nb), f32)
        for x in range(cx):
            wide[c, x * cy : (x + 1) * cy, x * nb : (x + 1) * nb] = table_y[c * cy : (c + 1) * cy, :]
        starts = [(r * cols_count + c) * run for r in range(rows_count)]
        block = jnp.concatenate([planes[at : at + run, :] for at in starts], axis=0)
        block = jnp.concatenate(
            [pltpu.roll(block, (LANES - i * cells) % LANES, 1) for i in range(sections)], axis=0
        )
        total = total + dot3(block[:, 0:cells], wide[c])
    for x in range(cx):
        tall[x * group : (x + 1) * group, :] = total[:, x * nb : (x + 1) * nb]
    spectrum = dot3(mix_x[...], tall[...])
    solved = []
    for k in range(depth):
        rows = slice(k * na, (k + 1) * na)
        solved.append(spectrum[rows] / (base[...] + lam_z[device * depth + k]))
    spectrum = jnp.concatenate(solved, axis=0)
    back = dot3(mix_x[...], spectrum, ((0,), (0,)))
    row = jnp.concatenate([back[x * group : (x + 1) * group] for x in range(cx)], axis=1)
    for c in range(cols_count):
        block = dot3(row, wide[c], ((1,), (1,)))
        for i in range(sections):
            for r in range(rows_count):
                at = (r * cols_count + c) * run
                start = (i * rows_count + r) * run
                out[at : at + run, i * cells : (i + 1) * cells] = block[start : start + run]
    for x in range(cx):
        for z in range(halves_z):
            save(x, z).wait()


def inverse_kernel(columns, table_high, table_low, out):
    cells = out.shape[0]
    turned = columns[...].T
    sections = [turned[i * cells : (i + 1) * cells] for i in range(LANES // cells)]
    turned = jnp.concatenate(sections, axis=1)
    out[...] = dot_halves(halves(turned), (table_high[...], table_low[...]))


smem = pl.BlockSpec(memory_space=pltpu.SMEM)
vmem = pl.BlockSpec(memory_space=pltpu.VMEM)
anywhere = pl.BlockSpec(memory_space=pl.ANY)
hbm = pl.BlockSpec(memory_space=pltpu.HBM)


def pick_group(total, most):
    best = 2
    for group in range(2, most + 1, 2):
        if total % group == 0:
            best = group
    return best


def local(
    species,
    velocity,
    diffusivity,
    divergence,
    log_rates,
    reactants,
    products,
    heat_weights,
    substeps,
):
    ns, cx, cy, nz = species.shape
    nr = log_rates.shape[0]
    rows_count = lax.axis_size("row")
    cols_count = lax.axis_size("col")
    device_count = rows_count * cols_count
    halves_z = nz // LANES
    ns8 = round_up(ns + 3, TILE)
    nr_rows = round_up(nr, 16)
    nr_lanes = round_up(nr, LANES)
    depth = nz // device_count
    cells = cx * cy
    dims = (ns, cx, cy, halves_z)

    codes = np.zeros((TILE, cells * halves_z), np.float32)
    inner_total = 0
    for x in range(cx):
        for y in range(cy):
            inside = 0 < x < cx - 1 and 0 < y < cy - 1
            if x in (0, cx - 1):
                slot, at = cx - 2 + (x > 0), y
            elif inside:
                slot, at = x - 1, y
            else:
                slot, at = cx + (y > 0), x
            for z in range(halves_z):
                block = (x * halves_z + z) * cy + y
                codes[0, block] = (x * cy + y) << 9 | slot << 4 | at << 1 | z
                codes[1, block] = 8.0 * inside
                inner_total += inside
    outer_total = cells * halves_z - inner_total
    inner_group = pick_group(inner_total, 12)
    outer_group = pick_group(outer_total, 14)

    def array(*shape, dtype=f32):
        return jax.ShapeDtypeStruct(shape, dtype)

    mv_shape = (cx + 2, halves_z, ns8 * TILE, LANES)
    estimate = pl.CostEstimate(flops=10**10, bytes_accessed=10**7, transcendentals=10**7)
    sp, row_a, row_b, col_a, col_b, speed, spread, rp, st, weight, order = pl.pallas_call(
        functools.partial(prepare_kernel, dims),
        out_shape=(
            array(halves_z, ns, cx, cy, LANES),
            *(array(ns, TILE, nz),) * 4,
            array(*velocity.shape),
            array(1, ns),
            array(nr_rows, LANES, dtype=bf16),
            array(2 * ns8, 2 * nr_lanes, dtype=bf16),
            array(ns8, LANES),
            array(1, cells * halves_z, dtype=jnp.int32),
        ),
        in_specs=[hbm] * 9,
        out_specs=(vmem,) * 11,
        scratch_shapes=[
            pltpu.VMEM((LANES, nr_lanes), f32),
            pltpu.VMEM((ns, nr), jnp.int32),
            pltpu.VMEM((ns, nr), jnp.int32),
            pltpu.VMEM((1, ns), f32),
            pltpu.VMEM(codes.shape, f32),
            pltpu.VMEM((1, nr), f32),
            pltpu.VMEM((cx, halves_z, cy), jnp.int32),
            pltpu.VMEM((cx * halves_z, LANES), f32),
            pltpu.SemaphoreType.DMA((cx, halves_z)),
            pltpu.SemaphoreType.DMA((8,)),
        ],
        compiler_params=pltpu.CompilerParams(vmem_limit_bytes=12 << 20),
        name="prepare",
    )(
        *(
            pltpu.with_memory_space_constraint(value, pltpu.HBM)
            for value in (
                species,
                velocity,
                diffusivity[None, :],
                reactants.T,
                products.T,
                heat_weights[None, :],
                jnp.asarray(codes),
                log_rates[None, :],
                substeps.transpose(0, 2, 1),
            )
        ),
    )
    sent = (row_a, row_b, col_a, col_b)

    def swap(value, axis, parity):
        pairs = []
        for low in range(parity, lax.axis_size(axis) - 1, 2):
            pairs += [(low, low + 1), (low + 1, low)]
        return lax.ppermute(value, axis, pairs)

    col_got = [swap(sent[2 + parity], "col", parity) for parity in range(2)]
    row_got = [swap(sent[parity], "row", parity) for parity in range(2)]
    got = (*row_got, *col_got)

    mv_all, heat = pl.pallas_call(
        functools.partial(inner_kernel, dims, inner_total, inner_group),
        out_shape=(array(*mv_shape), array(halves_z, cells, LANES)),
        in_specs=[smem, smem] + [vmem] * 5,
        out_specs=(vmem,) * 2,
        scratch_shapes=[
            pltpu.VMEM((ns8, inner_group * LANES), f32),
            pltpu.SMEM((MAXSUB + 2,), f32),
        ],
        compiler_params=pltpu.CompilerParams(vmem_limit_bytes=20 << 20),
        cost_estimate=estimate,
        name="inner",
    )(order, spread, sp, speed, rp, st, weight)
    sections = LANES // cells
    order_z = np.arange(nz).reshape(device_count, sections, depth // sections)
    order_z = order_z.transpose(1, 0, 2).reshape(nz)
    table_z = jnp.asarray(cosine_table(nz)[order_z])
    forward, mv_all, *table_parts = pl.pallas_call(
        functools.partial(
            outer_kernel, dims, inner_total, outer_total, outer_group, rows_count, cols_count
        ),
        out_shape=(
            array(nz // sections, LANES),
            array(*mv_shape),
            array(nz, nz, dtype=bf16),
            array(nz, nz, dtype=bf16),
        ),
        in_specs=[smem] * 2 + [vmem] * 8 + [anywhere] * 8,
        out_specs=(vmem,) * 4,
        scratch_shapes=[
            pltpu.VMEM((4, halves_z, ns, TILE, LANES), f32),
            pltpu.VMEM((ns8, outer_group * LANES), f32),
            pltpu.VMEM((halves_z, cells, LANES), f32),
            pltpu.SMEM((MAXSUB + 2,), f32),
            pltpu.SemaphoreType.DMA((4, halves_z)),
        ],
        input_output_aliases={4: 1},
        compiler_params=pltpu.CompilerParams(vmem_limit_bytes=20 << 20),
        cost_estimate=estimate,
        name="outer",
    )(
        order,
        spread,
        speed,
        divergence.reshape(cells, nz),
        mv_all,
        heat,
        rp,
        st,
        weight,
        table_z,
        *sent,
        *got,
    )
    dims = (rows_count, cols_count, depth, cx, cy)
    reacted, pressure = solve(forward, table_parts, mv_all, array(*species.shape), dims)
    return reacted, pressure.reshape(cx, cy, nz)


def solve(forward, table_parts, mv, reacted_shape, dims):
    rows_count, cols_count, depth, cx, cy = dims
    device_count = rows_count * cols_count
    nz = device_count * depth
    na, nb = rows_count * cx, cols_count * cy
    nb_pad = round_up(nb, LANES)
    sections = LANES // (cx * cy)
    run = depth // sections
    group = rows_count * depth

    def exchange(value):
        value = value.reshape(device_count, run, LANES)
        value = lax.all_to_all(value, ("row", "col"), split_axis=0, concat_axis=0, tiled=True)
        return value.reshape(device_count * run, LANES)

    table_y = np.zeros((nb, nb_pad), np.float32)
    table_y[:, :nb] = cosine_table(nb).T
    table_x = cosine_table(na).reshape(na, rows_count, cx)
    same = np.eye(depth, dtype=np.float32).reshape(depth, sections, run)
    mix_x = np.einsum("arx,kij->kaxirj", table_x, same)
    mix_x = mix_x.reshape(depth * na, cx * group)
    base = np.full((na, nb_pad), 1.0, np.float64)
    base[:, :nb] = screen + mode_values(na)[:, None] + mode_values(nb)[None, :]
    planes = exchange(forward)
    outgoing, reacted = pl.pallas_call(
        functools.partial(solve_kernel, dims),
        out_shape=(jax.ShapeDtypeStruct(planes.shape, f32), reacted_shape),
        in_specs=[smem, vmem, vmem, vmem, vmem, vmem],
        out_specs=(vmem, anywhere),
        scratch_shapes=[
            pltpu.VMEM((cols_count, cx * cy, cx * nb_pad), f32),
            pltpu.VMEM((cx * group, nb_pad), f32),
            pltpu.SemaphoreType.DMA((cx, mv.shape[1])),
        ],
        compiler_params=pltpu.CompilerParams(vmem_limit_bytes=16 << 20),
        name="solve",
    )(
        jnp.asarray(mode_values(nz).astype(np.float32)),
        planes,
        jnp.asarray(table_y),
        jnp.asarray(mix_x),
        jnp.asarray(base.astype(np.float32)),
        mv,
    )
    columns = exchange(outgoing)
    pressure = pl.pallas_call(
        inverse_kernel,
        out_shape=jax.ShapeDtypeStruct((cx * cy, nz), f32),
        in_specs=[vmem] * 3,
        out_specs=vmem,
        compiler_params=pltpu.CompilerParams(vmem_limit_bytes=4 << 20),
        name="inverse",
    )(columns, *table_parts)
    return reacted, pressure


def solution(mesh):
    return jax.shard_map(
        local,
        mesh=mesh,
        in_specs=(
            P(None, "row", "col", None),
            P(None, "row", "col", None),
            P(),
            P("row", "col", None),
            P(),
            P(),
            P(),
            P(),
            P("row", "col", None),
        ),
        out_specs=(P(None, "row", "col", None), P("row", "col", None)),
        check_vma=False,
    )
```

```python
import functools
import math

import jax
import jax.numpy as jnp
import numpy as np
from jax import lax
from jax.experimental import pallas as pl
from jax.experimental.pallas import tpu as pltpu
from jax.sharding import PartitionSpec as P

BLOCK = 128
MAXSUB = 6
LANES = 128
TILE = 8

time_step = 0.2
screen = 0.004
log2e = 1.4426950408889634
f32 = jnp.float32
bf16 = jnp.bfloat16


def round_up(value, multiple):
    return -(-value // multiple) * multiple


def cosine_table(length):
    wave = np.arange(length, dtype=np.float64)
    weight = np.where(wave == 0, math.sqrt(1.0 / length), math.sqrt(2.0 / length))
    table = weight[:, None] * np.cos(math.pi * wave[:, None] * (wave[None, :] + 0.5) / length)
    return table.astype(np.float32)


def mode_values(length):
    wave = np.arange(length, dtype=np.float64)
    return 2.0 - 2.0 * np.cos(math.pi * wave / length)


def halves(value):
    high = value.astype(bf16)
    return high, (value - high.astype(f32)).astype(bf16)


def dot_halves(left, right, dims=((1,), (0,))):
    def product(a, b):
        return lax.dot_general(a, b, (dims, ((), ())), preferred_element_type=f32)

    small = product(left[1], right[0]) + product(left[0], right[1])
    return product(left[0], right[0]) + small


def dot3(left, right, dims=((1,), (0,))):
    return dot_halves(halves(left), halves(right), dims)


def transport_weights(velocity):
    ups = [time_step * jnp.maximum(v, 0.0) for v in velocity]
    downs = [-time_step * jnp.minimum(v, 0.0) for v in velocity]
    own = 1.0
    for weight in ups + downs:
        own = own - weight
    return ups, downs, own


def z_neighbours(tiles):
    lane = lax.broadcasted_iota(jnp.int32, (TILE, LANES), 1)
    up = [pltpu.roll(t, 1, 1) for t in tiles]
    down = [pltpu.roll(t, LANES - 1, 1) for t in tiles]
    minus, plus = [], []
    last = len(tiles) - 1
    for i, tile in enumerate(tiles):
        minus.append(jnp.where(lane == 0, tile if i == 0 else up[i - 1], up[i]))
        plus.append(jnp.where(lane == LANES - 1, tile if i == last else down[i + 1], down[i]))
    return minus, plus


def sort_blocks(substeps, codes, inner_first):
    blocks = substeps.shape[1]
    square = (blocks, blocks)
    key = jnp.broadcast_to(substeps + inner_first, square)
    key_down = key.T
    down = lax.broadcasted_iota(jnp.int32, square, 0)
    across = lax.broadcasted_iota(jnp.int32, square, 1)
    ahead = (key_down > key) | ((key_down == key) & (down < across))
    rank = jnp.sum(jnp.where(ahead, 1.0, 0.0), axis=0, keepdims=True)
    rank_down = jnp.broadcast_to(rank, square).T
    value_down = jnp.broadcast_to(codes * 8.0 + substeps, square).T
    chosen = jnp.where(rank_down == across.astype(f32), value_down, 0.0)
    return jnp.sum(chosen, axis=0, keepdims=True).astype(jnp.int32)


def react_blocks(first_block, total, group, refs, target_of):
    order, steps, mv, conc, rp_ref, st_ref, heat, weight_ref = refs
    ns8 = conc.shape[0]
    pieces = st_ref.shape[1] // 2
    rows = rp_ref.shape[0]
    width = group * LANES

    def spread(row):
        return pl.ds(row, ns8, stride=TILE)

    def one_group(g, carry):
        base = first_block + g * group
        values = [order[0, base + i] for i in range(group)]
        ns = [value & 7 for value in values]
        hs = [steps[n] for n in ns]
        places = []
        for value in values:
            code = value >> 3
            places.append(((code >> 4) & 15, code & 1, (code >> 1) & 7, code >> 9))
        for i, (plane, half, row, _) in enumerate(places):
            conc[:, i * LANES : (i + 1) * LANES] = mv[plane, half, spread(row), :]

        def one_level(level, inner):
            held = conc[...]
            logs = jnp.log(held) * log2e
            high = logs.astype(bf16).astype(f32)
            low = logs - high
            fill = jnp.zeros((rp_ref.shape[1] - 2 * ns8, width), f32)
            stacked = jnp.concatenate([high, low, fill], axis=0).astype(bf16)
            rates = jnp.exp2(jnp.dot(rp_ref[...], stacked, preferred_element_type=f32))
            first, second = halves(rates)
            gap = jnp.zeros((pieces - rows, width), bf16)
            both = jnp.concatenate([first, gap, second, gap], axis=0)
            sums = jnp.dot(st_ref[...], both, preferred_element_type=f32)
            for i in range(group):
                part = slice(i * LANES, (i + 1) * LANES)
                old = held[:, part]
                fresh = old * (old + hs[i] * sums[:ns8, part]) / (old + hs[i] * sums[ns8:, part])
                conc[:, part] = jnp.where(ns[i] > level, fresh, old)
            return inner

        lax.fori_loop(0, ns[0], one_level, 0)
        for i, (plane, half, row, column) in enumerate(places):
            new = conc[:, i * LANES : (i + 1) * LANES]
            change = (new - mv[plane, half, spread(row), :]) * weight_ref[...]
            heat[half, pl.ds(column, 1), :] = jnp.sum(change, axis=0, keepdims=True)
            to_plane, to_row = target_of(plane, row)
            mv[to_plane, half, spread(to_row), :] = new
        return carry

    lax.fori_loop(0, total // group, one_group, 0)


def over_species(ns, body, unroll=18):
    def step(i, carry):
        for j in range(unroll):
            body(i * unroll + j)
        return carry

    lax.fori_loop(0, ns // unroll, step, 0)
    for s in range(ns - ns % unroll, ns):
        body(s)


def prepare_kernel(
    dims,
    species_hbm,
    velocity_hbm,
    diffusivity_hbm,
    reactants_hbm,
    products_hbm,
    weights_hbm,
    codes_hbm,
    rates_hbm,
    substeps_hbm,
    sp,
    row_a,
    row_b,
    col_a,
    col_b,
    velocity,
    diffusivity,
    rp_ref,
    st_ref,
    weight_ref,
    order_row,
    build,
    reactants,
    products,
    heat_weights,
    codes,
    log_rates,
    substeps,
    counts,
    in_sem,
    small_sem,
):
    ns, cx, cy, halves_z = dims
    nr = log_rates.shape[0]
    ns8 = weight_ref.shape[0]

    def load(x, z):
        return pltpu.make_async_copy(
            species_hbm.at[:, x, :, pl.ds(z * LANES, LANES)], sp.at[z, :, x], in_sem.at[x, z]
        )

    small = [
        pltpu.make_async_copy(source, target, small_sem.at[i])
        for i, (source, target) in enumerate(
            (
                (reactants_hbm, reactants),
                (products_hbm, products),
                (weights_hbm, heat_weights),
                (codes_hbm, codes),
                (diffusivity_hbm, diffusivity),
                (rates_hbm, log_rates),
                (substeps_hbm, substeps),
                (velocity_hbm, velocity),
            )
        )
    ]
    for copy in small[:-1]:
        copy.start()
    for x in range(cx):
        for z in range(halves_z):
            load(x, z).start()
    small[-1].start()
    for copy in small[:-1]:
        copy.wait()
    blocks = order_row.shape[1]
    counts[...] = jnp.zeros_like(counts)
    for x in range(cx):
        counts[x * halves_z : (x + 1) * halves_z, 0:cy] = substeps[x].astype(f32)
    down = lax.broadcasted_iota(jnp.int32, (LANES, blocks), 0)
    across = lax.broadcasted_iota(jnp.int32, (LANES, blocks), 1)
    repeat = jnp.where(lax.rem(across, cy) == down, 1.0, 0.0).astype(bf16)
    repeated = jnp.dot(counts[...].astype(bf16), repeat, preferred_element_type=f32)
    mine = lax.div(across, cy)[: counts.shape[0]] == down[: counts.shape[0]]
    flat_counts = jnp.sum(jnp.where(mine, repeated, 0.0), axis=0, keepdims=True)
    order_row[...] = sort_blocks(flat_counts, codes[0:1, :], codes[1:2, :])
    react = reactants[...].astype(f32)
    build[...] = jnp.zeros_like(build)
    build[0:ns, 0:nr] = react
    build[ns8 : ns8 + ns, 0:nr] = react
    rest = log_rates[...].reshape(1, nr) * log2e
    for i in range(3):
        piece = rest.astype(bf16).astype(f32)
        build[ns + i : ns + i + 1, 0:nr] = piece
        rest = rest - piece
    rp_ref[...] = build[...].T[: rp_ref.shape[0]].astype(bf16)
    build[...] = jnp.zeros_like(build)
    build[0:ns, 0:nr] = products[...].astype(f32)
    build[ns8 : ns8 + ns, 0:nr] = react
    half = build[0 : 2 * ns8, :].astype(bf16)
    st_ref[...] = jnp.concatenate([half, half], axis=1)
    build[:, 0:LANES] = jnp.zeros((build.shape[0], LANES), f32)
    build[:, 0:ns] = jnp.broadcast_to(heat_weights[...], (build.shape[0], ns))
    weight_ref[...] = build[:, 0:LANES].T[:ns8]

    row_even = lax.rem(lax.axis_index("row"), 2) == 0
    col_even = lax.rem(lax.axis_index("col"), 2) == 0
    x_a = jnp.where(row_even, cx - 1, 0)
    y_a = jnp.where(col_even, cy - 1, 0)
    flat = sp.reshape(halves_z, ns * cx * cy, LANES)
    for x in range(cx):
        for z in range(halves_z):
            load(x, z).wait()

    def body(s):
        for z in range(halves_z):
            q = slice(z * LANES, (z + 1) * LANES)
            row_a[s, :, q] = sp[z, s, x_a]
            row_b[s, :, q] = sp[z, s, cx - 1 - x_a]
            col_a[s, :, q] = flat[z, pl.ds(s * cx * cy + y_a, cx, stride=cy), :]
            col_b[s, :, q] = flat[z, pl.ds(s * cx * cy + cy - 1 - y_a, cx, stride=cy), :]

    over_species(ns, body)
    small[-1].wait()


def fill_steps(steps):
    steps[0] = 0.0
    for n in range(1, MAXSUB + 2):
        steps[n] = float(np.float32(time_step) / np.float32(n))


def inner_kernel(
    dims,
    total,
    group,
    order,
    diffusivity,
    sp,
    velocity,
    rp_ref,
    st_ref,
    weight_ref,
    mv,
    heat,
    conc,
    steps,
):
    ns, cx, cy, halves_z = dims
    ns8 = conc.shape[0]
    flat = sp.reshape(halves_z, ns * cx * cy, LANES)
    fill_steps(steps)
    mv[:, :, ns * TILE :, :] = jnp.full(
        (mv.shape[0], halves_z, (ns8 - ns) * TILE, LANES), 2.0, f32
    )
    heat[...] = jnp.zeros_like(heat)
    sublane = lax.broadcasted_iota(jnp.int32, (TILE, LANES), 0)

    def run_plane(slot, weights, tile_of):
        def body(s):
            d = time_step * diffusivity[0, s]
            got = [tile_of(s, z) for z in range(halves_z)]
            zm, zp = z_neighbours([g[0] for g in got])
            for z in range(halves_z):
                c = got[z][0]
                ups, downs, own = weights[z]
                sides = [*got[z][1:], zm[z], zp[z]]
                wanted = [ups[0], downs[0], ups[1], downs[1], ups[2], downs[2]]
                value = own * c
                near = -6.0 * c
                for w, t in zip(wanted, sides):
                    if t is None:
                        continue
                    value = value + w * t
                    near = near + t
                mv[slot, z, pl.ds(s * TILE, TILE), :] = value + d * near

        over_species(ns, body)

    lanes = [pl.ds(z * LANES, LANES) for z in range(halves_z)]
    for x in range(1, cx - 1):
        weights = [transport_weights([velocity[d, x, :, q] for d in range(3)]) for q in lanes]

        def tile_of(s, z, x=x):
            c = sp[z, s, x]
            return (
                c,
                sp[z, s, x - 1],
                sp[z, s, x + 1],
                pltpu.roll(c, 1, 0),
                pltpu.roll(c, TILE - 1, 0),
            )

        run_plane(x - 1, weights, tile_of)
    for slot, x, inward in ((cx - 2, 0, 1), (cx - 1, cx - 1, -1)):
        weights = []
        for q in lanes:
            ups, downs, own = transport_weights([velocity[d, x, :, q] for d in range(3)])
            weights.append((ups, downs, own))

        def tile_of(s, z, x=x, inward=inward):
            c = sp[z, s, x]
            inner = sp[z, s, x + inward]
            ym = jnp.where(sublane == 0, 0.0, pltpu.roll(c, 1, 0))
            yp = jnp.where(sublane == TILE - 1, 0.0, pltpu.roll(c, TILE - 1, 0))
            if inward > 0:
                return c, None, inner, ym, yp
            return c, inner, None, ym, yp

        run_plane(slot, weights, tile_of)
    for slot, y, inward in ((cx, 0, 1), (cx + 1, cy - 1, -1)):
        weights = []
        for q in lanes:
            rows = [
                jnp.concatenate([velocity[d, x, y : y + 1, q] for x in range(cx)], axis=0)
                for d in range(3)
            ]
            weights.append(transport_weights(rows))

        def tile_of(s, z, y=y, inward=inward):
            c = flat[z, pl.ds(s * cx * cy + y, cx, stride=cy), :]
            inner = flat[z, pl.ds(s * cx * cy + y + inward, cx, stride=cy), :]
            xm = pltpu.roll(c, 1, 0)
            xp = pltpu.roll(c, TILE - 1, 0)
            if inward > 0:
                return c, xm, xp, None, inner
            return c, xm, xp, inner, None

        run_plane(slot, weights, tile_of)
    refs = (order, steps, mv, conc, rp_ref, st_ref, heat, weight_ref)
    react_blocks(0, total, group, refs, lambda plane, row: (plane, row))


def outer_kernel(
    dims,
    first_block,
    total,
    group,
    rows_count,
    cols_count,
    order,
    diffusivity,
    velocity,
    divergence,
    mv_in,
    heat_inner,
    rp_ref,
    st_ref,
    weight_ref,
    table_z,
    row_sent_a,
    row_sent_b,
    col_sent_a,
    col_sent_b,
    row_got_a,
    row_got_b,
    col_got_a,
    col_got_b,
    forward,
    mv,
    table_high,
    table_low,
    halo,
    conc,
    heat,
    steps,
    halo_sem,
):
    ns, cx, cy, halves_z = dims
    fill_steps(steps)
    row = lax.axis_index("row")
    col = lax.axis_index("col")
    lanes = [pl.ds(z * LANES, LANES) for z in range(halves_z)]

    def fetch(source, side):
        for z, q in enumerate(lanes):
            pltpu.make_async_copy(source.at[:, :, q], halo.at[side, z], halo_sem.at[side, z]).start()

    for axis, (at, count, sent, got) in enumerate(
        (
            (row, rows_count, (row_sent_a, row_sent_b), (row_got_a, row_got_b)),
            (col, cols_count, (col_sent_a, col_sent_b), (col_got_a, col_got_b)),
        )
    ):
        even = lax.rem(at, 2) == 0
        for side, wall, kinds in (
            (2 * axis, at == 0, (1, 0)),
            (2 * axis + 1, at == count - 1, (0, 1)),
        ):
            for parity, kind in zip((even, jnp.logical_not(even)), kinds):
                pl.when(parity & wall)(functools.partial(fetch, sent[kind], side))
                pl.when(parity & jnp.logical_not(wall))(
                    functools.partial(fetch, got[kind], side)
                )
    sublane = lax.broadcasted_iota(jnp.int32, (TILE, LANES), 0)
    at_low = jnp.where(sublane == 0, 1.0, 0.0)
    at_high = jnp.where(sublane == TILE - 1, 1.0, 0.0)
    heat[...] = heat_inner[...]

    def arrive(side):
        for z, q in enumerate(lanes):
            pltpu.make_async_copy(
                row_got_a.at[:, :, q], halo.at[side, z], halo_sem.at[side, z]
            ).wait()

    for side in range(4):
        arrive(side)
    base = cx - 2
    for slot, x, y in ((2, None, 0), (3, None, cy - 1), (0, 0, None), (1, cx - 1, None)):
        weights = []
        for q in lanes:
            if y is None:
                ups, downs, _ = transport_weights([velocity[d, x, :, q] for d in range(2)])
                low = jnp.where(sublane == 0, ups[1], 0.0)
                high = jnp.where(sublane == TILE - 1, downs[1], 0.0)
                weights.append((ups[0] if slot == 0 else downs[0], low, high))
            else:
                across = jnp.concatenate([velocity[1, i, y : y + 1, q] for i in range(cx)], axis=0)
                ups, downs, _ = transport_weights([across])
                weights.append((ups[0] if slot == 2 else downs[0],))

        def body(s, slot=slot, x=x, y=y, weights=weights):
            d = time_step * diffusivity[0, s]
            for z in range(halves_z):
                rows = pl.ds(s * TILE, TILE)
                value = mv[base + slot, z, rows, :] + (weights[z][0] + d) * halo[slot, z, s]
                if y is None:
                    below = jnp.broadcast_to(halo[2, z, s, x : x + 1, :], (TILE, LANES))
                    above = jnp.broadcast_to(halo[3, z, s, x : x + 1, :], (TILE, LANES))
                    value = value + (weights[z][1] + d * at_low) * below
                    value = value + (weights[z][2] + d * at_high) * above
                mv[base + slot, z, rows, :] = value

        over_species(ns, body)

    def target_of(plane, at_row):
        ours = plane < base + 2
        edge = jnp.where(plane == base + 2, 0, cy - 1)
        return jnp.where(ours, plane, at_row - 1), jnp.where(ours, at_row, edge)

    refs = (order, steps, mv, conc, rp_ref, st_ref, heat, weight_ref)
    react_blocks(first_block, total, group, refs, target_of)

    heat_all = jnp.concatenate([heat[z] for z in range(halves_z)], axis=1)
    source = divergence[...] - heat_all / time_step
    table_high[...], table_low[...] = halves(table_z[...])
    result = dot_halves((table_high[...], table_low[...]), halves(source), ((1,), (1,)))
    rows = forward.shape[0]
    sections = [result[i * rows : (i + 1) * rows] for i in range(LANES // (cx * cy))]
    forward[...] = jnp.concatenate(sections, axis=1)


def solve_kernel(
    dims, lam_z, planes, table_y, mix_x, base, mv, out, reacted_hbm, wide, tall, out_sem
):
    rows_count, cols_count, depth, cx, cy = dims
    ns, halves_z = reacted_hbm.shape[0], mv.shape[1]
    tiles = mv.reshape(*mv.shape[:2], mv.shape[2] // TILE, TILE, LANES)

    def save(x, z):
        plane = {0: cx - 2, cx - 1: cx - 1}.get(x, x - 1)
        return pltpu.make_async_copy(
            tiles.at[plane, z, 0:ns],
            reacted_hbm.at[:, x, :, pl.ds(z * LANES, LANES)],
            out_sem.at[x, z],
        )

    for x in range(cx):
        for z in range(halves_z):
            save(x, z).start()
    cells = cx * cy
    nb = base.shape[1]
    na = rows_count * cx
    sections = LANES // cells
    run = depth // sections
    device = lax.axis_index("row") * cols_count + lax.axis_index("col")
    group = rows_count * depth
    total = jnp.zeros((group, cx * nb), f32)
    for c in range(cols_count):
        wide[c] = jnp.zeros((cells, cx * nb), f32)
        for x in range(cx):
            wide[c, x * cy : (x + 1) * cy, x * nb : (x + 1) * nb] = table_y[c * cy : (c + 1) * cy, :]
        starts = [(r * cols_count + c) * run for r in range(rows_count)]
        block = jnp.concatenate([planes[at : at + run, :] for at in starts], axis=0)
        block = jnp.concatenate(
            [pltpu.roll(block, (LANES - i * cells) % LANES, 1) for i in range(sections)], axis=0
        )
        total = total + dot3(block[:, 0:cells], wide[c])
    for x in range(cx):
        tall[x * group : (x + 1) * group, :] = total[:, x * nb : (x + 1) * nb]
    spectrum = dot3(mix_x[...], tall[...])
    solved = []
    for k in range(depth):
        rows = slice(k * na, (k + 1) * na)
        solved.append(spectrum[rows] / (base[...] + lam_z[device * depth + k]))
    spectrum = jnp.concatenate(solved, axis=0)
    back = dot3(mix_x[...], spectrum, ((0,), (0,)))
    row = jnp.concatenate([back[x * group : (x + 1) * group] for x in range(cx)], axis=1)
    for c in range(cols_count):
        block = dot3(row, wide[c], ((1,), (1,)))
        for i in range(sections):
            for r in range(rows_count):
                at = (r * cols_count + c) * run
                start = (i * rows_count + r) * run
                out[at : at + run, i * cells : (i + 1) * cells] = block[start : start + run]
    for x in range(cx):
        for z in range(halves_z):
            save(x, z).wait()


def inverse_kernel(columns, table_high, table_low, out):
    cells = out.shape[0]
    turned = columns[...].T
    sections = [turned[i * cells : (i + 1) * cells] for i in range(LANES // cells)]
    turned = jnp.concatenate(sections, axis=1)
    out[...] = dot_halves(halves(turned), (table_high[...], table_low[...]))


smem = pl.BlockSpec(memory_space=pltpu.SMEM)
vmem = pl.BlockSpec(memory_space=pltpu.VMEM)
anywhere = pl.BlockSpec(memory_space=pl.ANY)
hbm = pl.BlockSpec(memory_space=pltpu.HBM)


def pick_group(total, most):
    best = 2
    for group in range(2, most + 1, 2):
        if total % group == 0:
            best = group
    return best


def local(
    species,
    velocity,
    diffusivity,
    divergence,
    log_rates,
    reactants,
    products,
    heat_weights,
    substeps,
):
    ns, cx, cy, nz = species.shape
    nr = log_rates.shape[0]
    rows_count = lax.axis_size("row")
    cols_count = lax.axis_size("col")
    device_count = rows_count * cols_count
    halves_z = nz // LANES
    ns8 = round_up(ns + 3, TILE)
    nr_rows = round_up(nr, 16)
    nr_lanes = round_up(nr, LANES)
    depth = nz // device_count
    cells = cx * cy
    dims = (ns, cx, cy, halves_z)

    codes = np.zeros((TILE, cells * halves_z), np.float32)
    inner_total = 0
    for x in range(cx):
        for y in range(cy):
            inside = 0 < x < cx - 1 and 0 < y < cy - 1
            if x in (0, cx - 1):
                slot, at = cx - 2 + (x > 0), y
            elif inside:
                slot, at = x - 1, y
            else:
                slot, at = cx + (y > 0), x
            for z in range(halves_z):
                block = (x * halves_z + z) * cy + y
                codes[0, block] = (x * cy + y) << 9 | slot << 4 | at << 1 | z
                codes[1, block] = 8.0 * inside
                inner_total += inside
    outer_total = cells * halves_z - inner_total
    inner_group = pick_group(inner_total, 12)
    outer_group = pick_group(outer_total, 14)

    def array(*shape, dtype=f32):
        return jax.ShapeDtypeStruct(shape, dtype)

    mv_shape = (cx + 2, halves_z, ns8 * TILE, LANES)
    estimate = pl.CostEstimate(flops=10**10, bytes_accessed=10**7, transcendentals=10**7)
    sp, row_a, row_b, col_a, col_b, speed, spread, rp, st, weight, order = pl.pallas_call(
        functools.partial(prepare_kernel, dims),
        out_shape=(
            array(halves_z, ns, cx, cy, LANES),
            *(array(ns, TILE, nz),) * 4,
            array(*velocity.shape),
            array(1, ns),
            array(nr_rows, LANES, dtype=bf16),
            array(2 * ns8, 2 * nr_lanes, dtype=bf16),
            array(ns8, LANES),
            array(1, cells * halves_z, dtype=jnp.int32),
        ),
        in_specs=[hbm] * 9,
        out_specs=(vmem,) * 11,
        scratch_shapes=[
            pltpu.VMEM((LANES, nr_lanes), f32),
            pltpu.VMEM((ns, nr), jnp.int32),
            pltpu.VMEM((ns, nr), jnp.int32),
            pltpu.VMEM((1, ns), f32),
            pltpu.VMEM(codes.shape, f32),
            pltpu.VMEM((nr,), f32),
            pltpu.VMEM((cx, halves_z, cy), jnp.int32),
            pltpu.VMEM((cx * halves_z, LANES), f32),
            pltpu.SemaphoreType.DMA((cx, halves_z)),
            pltpu.SemaphoreType.DMA((8,)),
        ],
        compiler_params=pltpu.CompilerParams(vmem_limit_bytes=12 << 20),
        name="prepare",
    )(
        *(
            pltpu.with_memory_space_constraint(value, pltpu.HBM)
            for value in (
                species,
                velocity,
                diffusivity[None, :],
                reactants.T,
                products.T,
                heat_weights[None, :],
                jnp.asarray(codes),
                log_rates,
                substeps.transpose(0, 2, 1),
            )
        ),
    )
    sent = (row_a, row_b, col_a, col_b)

    def swap(value, axis, parity):
        pairs = []
        for low in range(parity, lax.axis_size(axis) - 1, 2):
            pairs += [(low, low + 1), (low + 1, low)]
        return lax.ppermute(value, axis, pairs)

    col_got = [swap(sent[2 + parity], "col", parity) for parity in range(2)]
    row_got = [swap(sent[parity], "row", parity) for parity in range(2)]
    got = (*row_got, *col_got)

    mv_all, heat = pl.pallas_call(
        functools.partial(inner_kernel, dims, inner_total, inner_group),
        out_shape=(array(*mv_shape), array(halves_z, cells, LANES)),
        in_specs=[smem, smem] + [vmem] * 5,
        out_specs=(vmem,) * 2,
        scratch_shapes=[
            pltpu.VMEM((ns8, inner_group * LANES), f32),
            pltpu.SMEM((MAXSUB + 2,), f32),
        ],
        compiler_params=pltpu.CompilerParams(vmem_limit_bytes=20 << 20),
        cost_estimate=estimate,
        name="inner",
    )(order, spread, sp, speed, rp, st, weight)
    sections = LANES // cells
    order_z = np.arange(nz).reshape(device_count, sections, depth // sections)
    order_z = order_z.transpose(1, 0, 2).reshape(nz)
    table_z = jnp.asarray(cosine_table(nz)[order_z])
    forward, mv_all, *table_parts = pl.pallas_call(
        functools.partial(
            outer_kernel, dims, inner_total, outer_total, outer_group, rows_count, cols_count
        ),
        out_shape=(
            array(nz // sections, LANES),
            array(*mv_shape),
            array(nz, nz, dtype=bf16),
            array(nz, nz, dtype=bf16),
        ),
        in_specs=[smem] * 2 + [vmem] * 8 + [anywhere] * 8,
        out_specs=(vmem,) * 4,
        scratch_shapes=[
            pltpu.VMEM((4, halves_z, ns, TILE, LANES), f32),
            pltpu.VMEM((ns8, outer_group * LANES), f32),
            pltpu.VMEM((halves_z, cells, LANES), f32),
            pltpu.SMEM((MAXSUB + 2,), f32),
            pltpu.SemaphoreType.DMA((4, halves_z)),
        ],
        input_output_aliases={4: 1},
        compiler_params=pltpu.CompilerParams(vmem_limit_bytes=20 << 20),
        cost_estimate=estimate,
        name="outer",
    )(
        order,
        spread,
        speed,
        divergence.reshape(cells, nz),
        mv_all,
        heat,
        rp,
        st,
        weight,
        table_z,
        *sent,
        *got,
    )
    dims = (rows_count, cols_count, depth, cx, cy)
    reacted, pressure = solve(forward, table_parts, mv_all, array(*species.shape), dims)
    return reacted, pressure.reshape(cx, cy, nz)


def solve(forward, table_parts, mv, reacted_shape, dims):
    rows_count, cols_count, depth, cx, cy = dims
    device_count = rows_count * cols_count
    nz = device_count * depth
    na, nb = rows_count * cx, cols_count * cy
    nb_pad = round_up(nb, LANES)
    sections = LANES // (cx * cy)
    run = depth // sections
    group = rows_count * depth

    def exchange(value):
        value = value.reshape(device_count, run, LANES)
        value = lax.all_to_all(value, ("row", "col"), split_axis=0, concat_axis=0, tiled=True)
        return value.reshape(device_count * run, LANES)

    table_y = np.zeros((nb, nb_pad), np.float32)
    table_y[:, :nb] = cosine_table(nb).T
    table_x = cosine_table(na).reshape(na, rows_count, cx)
    same = np.eye(depth, dtype=np.float32).reshape(depth, sections, run)
    mix_x = np.einsum("arx,kij->kaxirj", table_x, same)
    mix_x = mix_x.reshape(depth * na, cx * group)
    base = np.full((na, nb_pad), 1.0, np.float64)
    base[:, :nb] = screen + mode_values(na)[:, None] + mode_values(nb)[None, :]
    planes = exchange(forward)
    outgoing, reacted = pl.pallas_call(
        functools.partial(solve_kernel, dims),
        out_shape=(jax.ShapeDtypeStruct(planes.shape, f32), reacted_shape),
        in_specs=[smem, vmem, vmem, vmem, vmem, vmem],
        out_specs=(vmem, anywhere),
        scratch_shapes=[
            pltpu.VMEM((cols_count, cx * cy, cx * nb_pad), f32),
            pltpu.VMEM((cx * group, nb_pad), f32),
            pltpu.SemaphoreType.DMA((cx, mv.shape[1])),
        ],
        compiler_params=pltpu.CompilerParams(vmem_limit_bytes=16 << 20),
        name="solve",
    )(
        jnp.asarray(mode_values(nz).astype(np.float32)),
        planes,
        jnp.asarray(table_y),
        jnp.asarray(mix_x),
        jnp.asarray(base.astype(np.float32)),
        mv,
    )
    columns = exchange(outgoing)
    pressure = pl.pallas_call(
        inverse_kernel,
        out_shape=jax.ShapeDtypeStruct((cx * cy, nz), f32),
        in_specs=[vmem] * 3,
        out_specs=vmem,
        compiler_params=pltpu.CompilerParams(vmem_limit_bytes=4 << 20),
        name="inverse",
    )(columns, *table_parts)
    return reacted, pressure


def solution(mesh):
    return jax.shard_map(
        local,
        mesh=mesh,
        in_specs=(
            P(None, "row", "col", None),
            P(None, "row", "col", None),
            P(),
            P("row", "col", None),
            P(),
            P(),
            P(),
            P(),
            P("row", "col", None),
        ),
        out_specs=(P(None, "row", "col", None), P("row", "col", None)),
        check_vma=False,
    )
```
